32 devices in a mesh: row: 8 (over z, core), col: 4 (over y, x).
Axes of the slice: x: 2, y: 2, z: 4, core: 2. Of those that a mesh axis runs over, the one named last changes fastest.
Arguments:
- context: bfloat16 [128, 16384], P('row', 'col'), may hold values from -6 to 6
- out_weight: bfloat16 [16384, 16384], P('col', 'row'), may hold values from -0.046875 to 0.046875
- residual: bfloat16 [128, 16384], P('col', 'row'), may hold values from -80 to 80
- teacher_gain: float32 [16384], replicated, may hold values from 0.5 to 1.5
- student_hidden: bfloat16 [128, 4096], P(('row', 'col')), may hold values from -6 to 6
- student_gain: float32 [4096], replicated, may hold values from 0.5 to 1.5
- projector: bfloat16 [4096, 16384], P(None, ('row', 'col')), may hold values from -0.09375 to 0.09375
Outputs:
- grad_proj: float32 [4096, 16384], P(None, ('row', 'col'))
- grad_gain: float32 [4096], replicated
- loss: float32 [], replicated
The draws below stay inside these ranges and needn't reach their ends.
All inputs are finite; a program needn't handle non-finite values.
Results may differ from the reference program's by a relative error of at most 0.0065.
Values may be sent and summed in bfloat16 or wider, within the bound.
A program may use at most 64 MiB of HBM per device.

```python
import math
import jax
import jax.numpy as jnp
from jax import lax

D_T = 16384
D_S = 4096
TOKENS = 128


def draw_residual(key, part):
    keys = jax.random.split(key, 3)
    ramp = jnp.exp(jnp.linspace(0.0, math.log(3.0), D_T))
    column = ramp * jnp.exp(jax.random.uniform(keys[1], (D_T,), minval=0.0, maxval=math.log(2.0)))
    rowwise = jnp.exp(jax.random.uniform(keys[2], (TOKENS, 1), minval=0.0, maxval=math.log(4.0)))
    base = jnp.clip(jax.random.normal(keys[0], (TOKENS, D_T)), -6.0, 6.0)
    return (base * rowwise * column * 0.5).astype(jnp.bfloat16)


def block_scale(own_key, dims, cuts, smallest, largest):
    level = 1.0
    for dim, blocks in cuts:
        heights = jax.random.uniform(jax.random.fold_in(jax.random.fold_in(own_key, 6), dim), (blocks,), jnp.float32, smallest / len(cuts), largest / len(cuts))
        level = level * jnp.repeat(jnp.exp(heights), dims[dim] // blocks).reshape((-1,) + (1,) * (len(dims) - 1 - dim))
    return level


def normal_values(stream_key, dims, deviation, bound, pieces=(), held_as=jnp.bfloat16):
    result = deviation * jax.random.normal(stream_key, dims, jnp.float32)
    if pieces:
        result = result * block_scale(stream_key, dims, pieces, -0.22, 0.18)
    return jnp.clip(result, -bound, bound).astype(held_as)


def setup_inputs(seed: int = 0) -> dict:
    seeds = jax.random.split(jax.random.key(seed), 8)
    return {
        "context": normal_values(seeds[0], (TOKENS, D_T), 1.0, 6.0, ((0, 8), (1, 4))),
        "out_weight": normal_values(seeds[1], (D_T, D_T), D_T ** -0.5, 0.046875, ((0, 4), (1, 8))),
        "residual": draw_residual(jax.random.fold_in(seeds[7], 71), 0),
        "teacher_gain": jnp.clip(jax.random.uniform(seeds[3], (D_T,), jnp.float32, 0.5, 1.5), 0.5, 1.5),
        "student_hidden": normal_values(seeds[4], (TOKENS, D_S), 1.0, 6.0, ((0, 32),)),
        "student_gain": jnp.clip(jax.random.uniform(seeds[5], (D_S,), jnp.float32, 0.5, 1.5), 0.5, 1.5),
        "projector": normal_values(seeds[6], (D_S, D_T), D_S ** -0.5, 0.09375, ((1, 32),)),
    }


norm_eps = 1e-05

def reference(context, out_weight, residual, teacher_gain, student_hidden, student_gain, projector):
    teacher_sum = jnp.dot(context, out_weight, preferred_element_type=jnp.float32) + residual.astype(jnp.float32)
    squares = lax.optimization_barrier(jnp.mean(teacher_sum * teacher_sum, axis=1, keepdims=True))
    target = (teacher_sum * lax.rsqrt(squares + norm_eps) * teacher_gain).astype(jnp.bfloat16)
    widened = student_hidden.astype(jnp.float32)
    normed = widened * lax.rsqrt(lax.optimization_barrier(jnp.mean(widened * widened, axis=1, keepdims=True)) + norm_eps)
    student_out = (normed * student_gain).astype(jnp.bfloat16)
    predicted = jnp.dot(student_out, projector, preferred_element_type=jnp.float32)
    difference = predicted - target.astype(jnp.float32)
    loss = jnp.sum(difference * difference) / (TOKENS * D_T)
    error_term = (difference * (1.0 / 64.0)).astype(jnp.bfloat16)
    grad_proj = jnp.dot(student_out.T, error_term, preferred_element_type=jnp.float32)
    grad_normed = jnp.dot(error_term, projector.T, preferred_element_type=jnp.float32)
    grad_gain = lax.optimization_barrier(jnp.sum(grad_normed * normed, axis=0))
    return (grad_proj, grad_gain, loss)
```

```python
import functools

import jax
import jax.numpy as jnp
from jax import lax
from jax.experimental import pallas as pl
from jax.experimental.pallas import tpu as pltpu
from jax.sharding import PartitionSpec as P

norm_eps = 1e-05
LANES = 128
CHUNKS = 4
HIDDEN_AT = 2
AHEAD = 3
MESH = pl.DeviceIdType.MESH


def to_row(column):
    return jnp.transpose(jnp.broadcast_to(column, (LANES, LANES)))[0:1, :]


def to_column(row):
    return jnp.transpose(jnp.broadcast_to(row, (LANES, LANES)))[:, 0:1]


def body(
    n_row, n_col,
    context, weight, residual, teacher_gain, hidden, student_gain, projector,
    student_out, error_out, gain_out, loss_out,
    student, error, ctx, w, proj, acc, part_out, part_in, res, hid, wide, sgain, tgain,
    predicted, total, sq_out, sq_in, gp, gp_in, gg_out, gg,
    local_sem, w_sem, ctx_send, ctx_recv, hid_chain, hid_partner, hid_col, hid_recv,
    col_send, col_recv, all_send, all_recv,
):
    devices = n_row * n_col
    chips = n_row // 2
    r, c = lax.axis_index("row"), lax.axis_index("col")
    me = r * n_col + c
    p, core = r // 2, r % 2
    tok = context.shape[0]
    features = context.shape[1]
    chunk = features // CHUNKS
    tokens = tok * n_row
    width = proj.shape[1]
    res_rows = residual.shape[0]
    hid_rows = hidden.shape[0]
    d_s = hidden.shape[1]
    d_t = width * devices
    segments = gain_out.shape[0]
    repeat = devices // segments

    def rows_of(row):
        return pl.ds(pl.multiple_of(row * tok, tok), tok)

    def row_of(pos):
        return pos * 2 + core

    own = [
        pltpu.make_async_copy(context, ctx.at[rows_of(r), :], local_sem.at[0]),
        pltpu.make_async_copy(hidden, hid.at[me], local_sem.at[1]),
        pltpu.make_async_copy(
            residual.at[:, pl.ds(pl.multiple_of(c * width, width), width)],
            res.at[pl.ds(pl.multiple_of(c * res_rows, res_rows), res_rows), :],
            local_sem.at[2],
        ),
    ]
    for copy in own:
        copy.start()

    def w_copy(k):
        part = pl.ds(k * chunk, chunk)
        return pltpu.make_async_copy(weight.at[part, :], w.at[part, :], w_sem.at[k])

    for k in range(CHUNKS):
        w_copy(k).start()
    proj_copy = pltpu.make_async_copy(projector, proj, local_sem.at[3])
    proj_copy.start()

    barrier = pltpu.get_barrier_semaphore()

    up, down, partner = (r + 2, c), (r - 2, c), (r + 1 - 2 * core, c)
    targets = {0: up, 1: down, 2: partner}

    def ctx_copy(pos, k, way, first=False):
        row = row_of(pos)
        cols = pl.ds(k * chunk, chunk)
        there = ctx.at[rows_of(row), cols]
        return pltpu.make_async_remote_copy(
            src_ref=context.at[:, cols] if first else there,
            dst_ref=there,
            send_sem=ctx_send.at[way, pos, k],
            recv_sem=ctx_recv.at[row, k],
            device_id=targets[way],
            device_id_type=MESH,
        )

    def hid_copy(row, col, device, send_sem, first=False):
        slot = row * n_col + col
        return pltpu.make_async_remote_copy(
            src_ref=hidden if first else hid.at[slot],
            dst_ref=hid.at[slot],
            send_sem=send_sem,
            recv_sem=hid_recv.at[slot],
            device_id=device,
            device_id_type=MESH,
        )

    def hid_way(pos, way, first=False):
        return hid_copy(row_of(pos), c, targets[way], hid_chain.at[way, pos], first)

    def hid_side(pos, i, first=False):
        return hid_copy(row_of(pos), c, (r, (c + 1 + i) % n_col), hid_col.at[i, pos], first)

    def hid_cross(pos, i):
        col = (c + 1 + i) % n_col
        return hid_copy(row_of(pos), col, partner, hid_partner.at[i, pos])

    def res_copy(i):
        j = (c + 1 + i) % n_col
        return pltpu.make_async_remote_copy(
            src_ref=residual.at[:, pl.ds(pl.multiple_of(j * width, width), width)],
            dst_ref=res.at[pl.ds(pl.multiple_of(c * res_rows, res_rows), res_rows), :],
            send_sem=col_send.at[0, i],
            recv_sem=col_recv.at[0, c],
            device_id=(r, j),
            device_id_type=MESH,
        )

    has_up, has_down = p < chips - 1, p > 0

    def greet(device):
        pl.semaphore_signal(barrier, inc=1, device_id=device, device_id_type=MESH)

    @pl.when(has_up)
    def _():
        greet(up)

    @pl.when(has_down)
    def _():
        greet(down)

    greet(partner)
    for i in range(n_col - 1):
        greet((r, (c + 1 + i) % n_col))
    peers = n_col + has_up.astype(jnp.int32) + has_down.astype(jnp.int32)
    pl.semaphore_wait(barrier, peers)

    def each_way(guard_up, guard_down, fn):
        @pl.when(guard_up)
        def _():
            fn(0)

        @pl.when(guard_down)
        def _():
            fn(1)

    def own_chunk(k):
        each_way(has_up, has_down, lambda way: ctx_copy(p, k, way, True).start())
        ctx_copy(p, k, 2, True).start()

    for k in range(AHEAD):
        own_chunk(k)
    for i in range(n_col - 1):
        hid_side(p, i, True).start()
        res_copy(i).start()
    hid_way(p, 2, True).start()

    def arrive_hid(pos, way, onward):
        hid_way(pos, way).wait_recv()

        @pl.when(onward)
        def _():
            hid_way(pos, way).start()

        hid_way(pos, 2).start()
        for i in range(n_col - 1):
            hid_side(pos, i).start()

    def arrive_ctx(pos, k, way, onward):
        ctx_copy(pos, k, way).wait_recv()

        @pl.when(onward)
        def _():
            ctx_copy(pos, k, way).start()

        ctx_copy(pos, k, 2).start()

    def both(distance, fn):
        @pl.when(p >= distance)
        def _():
            fn(p - distance, 0, has_up)

        @pl.when(p + distance < chips)
        def _():
            fn(p + distance, 1, has_down)

    own[0].wait()

    def product(j, k):
        cols = pl.ds(pl.multiple_of(j * width, width), width)
        return jnp.dot(
            ctx[:, k * chunk:(k + 1) * chunk],
            w[k * chunk:(k + 1) * chunk, cols],
            preferred_element_type=jnp.float32,
        )

    def part_copy(i):
        j = (c + 1 + i) % n_col
        return pltpu.make_async_remote_copy(
            src_ref=part_out.at[i],
            dst_ref=part_in.at[c],
            send_sem=col_send.at[1, i],
            recv_sem=col_recv.at[1, c],
            device_id=(r, j),
            device_id_type=MESH,
        )

    def multiply(k):
        for pos in range(chips):
            row = pos * 2 + 1 - core
            there = ctx.at[rows_of(row), pl.ds(k * chunk, chunk)]
            pltpu.make_async_remote_copy(
                src_ref=there, dst_ref=there, send_sem=ctx_send.at[2, pos, k],
                recv_sem=ctx_recv.at[row, k], device_id=partner, device_id_type=MESH,
            ).wait_recv()
        w_copy(k).wait()
        if k < CHUNKS - 1:
            def step(j, _, k=k):
                if k == 0:
                    acc[j] = product(j, k)
                else:
                    acc[j] += product(j, k)
                return 0

            lax.fori_loop(0, n_col, step, 0)
        else:
            def last(i, _):
                j = (c + 1 + i) % n_col
                part_out[i] = (acc[j] + product(j, CHUNKS - 1)).astype(jnp.bfloat16)
                part_copy(i).start()
                return 0

            lax.fori_loop(0, n_col - 1, last, 0)
            acc[c] = acc[c] + product(c, CHUNKS - 1)

    for wave in range(1, CHUNKS + chips - 1):
        if wave >= chips:
            multiply(wave - chips)
        for distance in range(1, chips):
            k = wave - distance
            if 0 <= k < CHUNKS:
                both(distance, lambda pos, way, on: arrive_ctx(pos, k, way, on))
            if k == HIDDEN_AT:
                both(distance, arrive_hid)
        if AHEAD - 1 + wave < CHUNKS:
            own_chunk(AHEAD - 1 + wave)
        if wave == max(HIDDEN_AT, 1):
            each_way(has_up, has_down, lambda way: hid_way(p, way, True).start())
    multiply(CHUNKS - 1)

    for pos in range(chips):
        for i in range(n_col - 1):
            j = (c + 1 + i) % n_col
            hid_copy(row_of(pos), j, (r, j), hid_col.at[i, pos]).wait_recv()
            hid_cross(pos, i).start()
    for j in range(student_gain.shape[0]):
        sgain[:, j * LANES:(j + 1) * LANES] = student_gain[j:j + 1, :]
    gain_rows = width // LANES
    for j in range(gain_rows):
        tgain[:, j * LANES:(j + 1) * LANES] = teacher_gain[pl.ds(me * gain_rows + j, 1), :]
    for pos in range(chips):
        for j in range(n_col):
            hid_copy(pos * 2 + 1 - core, j, partner, hid_chain.at[2, pos]).wait_recv()
    own[1].wait()

    group = 8 // hid_rows if hid_rows < 8 else 1

    def widen(s, _):
        wide_rows = pl.ds(pl.multiple_of(s * group * hid_rows, 8), group * hid_rows)
        wide[wide_rows, :] = jnp.concatenate(
            [hid[s * group + i].astype(jnp.float32) for i in range(group)], axis=0
        )
        return 0

    lax.fori_loop(0, devices // group, widen, 0)

    tile = 16

    def normalize(t, _):
        rows = pl.ds(pl.multiple_of(t * tile, tile), tile)
        x = wide[rows, :]
        normed = x * lax.rsqrt(jnp.mean(x * x, axis=1, keepdims=True) + norm_eps)
        wide[rows, :] = normed
        student[rows, :] = (normed * sgain[...]).astype(jnp.bfloat16)
        return 0

    lax.fori_loop(0, tokens // tile, normalize, 0)
    student_copy = pltpu.make_async_copy(student, student_out, local_sem.at[4])
    student_copy.start()
    proj_copy.wait()
    predicted[...] = jnp.dot(student[...], proj[...], preferred_element_type=jnp.float32)

    own[2].wait()
    for i in range(n_col - 1):
        j = (c + 1 + i) % n_col
        pltpu.make_async_remote_copy(
            src_ref=part_out.at[i], dst_ref=part_in.at[j], send_sem=col_send.at[1, i],
            recv_sem=col_recv.at[1, j], device_id=(r, j), device_id_type=MESH,
        ).wait_recv()
        rows = res.at[pl.ds(pl.multiple_of(j * res_rows, res_rows), res_rows), :]
        pltpu.make_async_remote_copy(
            src_ref=rows, dst_ref=rows, send_sem=col_send.at[0, i],
            recv_sem=col_recv.at[0, j], device_id=(r, j), device_id_type=MESH,
        ).wait_recv()
    summed = acc[c] + res[...].astype(jnp.float32)
    for i in range(n_col - 1):
        summed = summed + part_in[(c + 1 + i) % n_col].astype(jnp.float32)
    total[...] = summed
    squares = jnp.sum(summed * summed, axis=1, keepdims=True)
    for b in range(tokens // LANES):
        lanes = slice(b * LANES, (b + 1) * LANES)
        row = to_row(squares[lanes, :])
        sq_out[:, lanes] = row
        sq_in[me, :, lanes] = row

    def to_all(stage, src, dst):
        def copy(i):
            d = (me + 1 + i) % devices
            return pltpu.make_async_remote_copy(
                src_ref=src(d), dst_ref=dst.at[me],
                send_sem=all_send.at[stage], recv_sem=all_recv.at[stage],
                device_id=(d // n_col, d % n_col), device_id_type=MESH,
            )

        def send(i, _):
            copy(i).start()
            return 0

        lax.fori_loop(0, devices - 1, send, 0)

    def wait_all(sem, stage, dst):
        view = dst.at[pl.ds(0, devices - 1)]
        pltpu.make_async_copy(view, view, sem.at[stage]).wait()

    to_all(0, lambda d: sq_out, sq_in)
    wait_all(all_recv, 0, sq_in)
    sums = jnp.sum(sq_in[...], axis=0)
    factor = lax.rsqrt(sums / d_t + norm_eps)
    loss_part = jnp.zeros((1, 1), jnp.float32)
    for b in range(tokens // LANES):
        rows = slice(b * LANES, (b + 1) * LANES)
        target = (total[rows, :] * to_column(factor[:, rows]) * tgain[...]).astype(jnp.bfloat16)
        difference = predicted[rows, :] - target.astype(jnp.float32)
        loss_part = loss_part + jnp.sum(difference * difference, keepdims=True)
        error[rows, :] = (difference * (1.0 / 64.0)).astype(jnp.bfloat16)

    error_copy = pltpu.make_async_copy(error, error_out, local_sem.at[5])
    error_copy.start()

    block = 512

    def gain_step(n, _):
        rows = pl.ds(pl.multiple_of(n * block, block), block)
        grad_normed = lax.dot_general(
            error[...], proj[rows, :], (((1,), (1,)), ((), ())),
            preferred_element_type=jnp.float32,
        )
        part = jnp.sum(grad_normed * wide[:, rows], axis=0, keepdims=True)
        for q in range(block // LANES):
            gp[n * (block // LANES) + q, 0:1, :] = part[:, q * LANES:(q + 1) * LANES]
            gp[n * (block // LANES) + q, 1:2, :] = jnp.broadcast_to(loss_part, (1, LANES))
        return 0

    lax.fori_loop(0, d_s // block, gain_step, 0)
    gp_in[me] = gp[me // repeat]
    to_all(1, lambda d: gp.at[d // repeat], gp_in)
    wait_all(all_recv, 1, gp_in)
    both_sums = jnp.sum(gp_in[...], axis=0)
    gg_out[...] = both_sums[0:1, :]
    gg[me] = both_sums[0:1, :]
    to_all(2, lambda d: gg_out, gg)
    loss_out[...] = both_sums[1:2, :] / (tokens * d_t)
    wait_all(all_recv, 2, gg)
    for j in range(segments):
        gain_out[j:j + 1, :] = gg[j * repeat]

    student_copy.wait()
    error_copy.wait()
    each_way(has_up, has_down, lambda way: hid_way(p, way).wait_send())
    hid_way(p, 2).wait_send()
    for k in range(CHUNKS):
        each_way(has_up, has_down, lambda way: ctx_copy(p, k, way).wait_send())
        ctx_copy(p, k, 2).wait_send()
    for i in range(n_col - 1):
        hid_side(p, i).wait_send()
        res_copy(i).wait_send()
        part_copy(i).wait_send()

    def left(pos, way, onward):
        @pl.when(onward)
        def _():
            hid_way(pos, way).wait_send()
            for k in range(CHUNKS):
                ctx_copy(pos, k, way).wait_send()

        hid_way(pos, 2).wait_send()
        for k in range(CHUNKS):
            ctx_copy(pos, k, 2).wait_send()
        for i in range(n_col - 1):
            hid_side(pos, i).wait_send()

    for distance in range(1, chips):
        both(distance, left)
    for pos in range(chips):
        for i in range(n_col - 1):
            hid_cross(pos, i).wait_send()
    wait_all(all_send, 0, sq_in)
    wait_all(all_send, 1, gp_in)
    wait_all(all_send, 2, gg)


def project(student_in, error_in, gain_in, loss_in, grad_out, gain_out, loss_out,
            student, error, grad, in_sem, out_sem):
    n, _, step = student.shape
    error_copy = pltpu.make_async_copy(error_in, error, in_sem.at[n])
    error_copy.start()

    def fetch(i):
        cols = pl.ds(pl.multiple_of(i * step, step), step)
        return pltpu.make_async_copy(student_in.at[:, cols], student.at[i], in_sem.at[i])

    def write(i):
        rows = pl.ds(pl.multiple_of(i * step, step), step)
        return pltpu.make_async_copy(grad.at[i], grad_out.at[rows, :], out_sem.at[i])

    for i in range(n):
        fetch(i).start()
    small = [
        pltpu.make_async_copy(gain_in, gain_out, in_sem.at[n + 1]),
        pltpu.make_async_copy(loss_in, loss_out, in_sem.at[n + 2]),
    ]
    for copy in small:
        copy.start()
    error_copy.wait()

    def block(i, _):
        fetch(i).wait()
        grad[i] = lax.dot_general(
            student[i], error[...], (((0,), (0,)), ((), ())), preferred_element_type=jnp.float32
        )
        write(i).start()
        return 0

    lax.fori_loop(0, n, block, 0)
    for i in range(n):
        write(i).wait()
    for copy in small:
        copy.wait()


def project_call(student_all, error_term, gain, loss):
    tokens, d_s = student_all.shape
    width = error_term.shape[1]
    steps = 8
    rows = d_s // steps
    hbm = pl.BlockSpec(memory_space=pltpu.HBM)
    f32, bf16 = jnp.float32, jnp.bfloat16
    return pl.pallas_call(
        project,
        out_shape=(
            jax.ShapeDtypeStruct((d_s, width), f32),
            jax.ShapeDtypeStruct(gain.shape, f32),
            jax.ShapeDtypeStruct(loss.shape, f32),
        ),
        in_specs=[hbm] * 4,
        out_specs=(hbm,) * 3,
        scratch_shapes=[
            pltpu.VMEM((steps, tokens, rows), bf16),
            pltpu.VMEM((tokens, width), bf16),
            pltpu.VMEM((steps, rows, width), f32),
            pltpu.SemaphoreType.DMA((steps + 3,)),
            pltpu.SemaphoreType.DMA((steps,)),
        ],
        compiler_params=pltpu.CompilerParams(vmem_limit_bytes=67_000_000),
    )(student_all, error_term, gain, loss)


def per_device(
    n_row, n_col,
    context, out_weight, residual, teacher_gain, student_hidden, student_gain, projector,
):
    devices = n_row * n_col
    chips = n_row // 2
    tokens = context.shape[0] * n_row
    d_s, width = projector.shape
    segments = min(devices, d_s // LANES)
    f32, bf16 = jnp.float32, jnp.bfloat16
    anywhere = pl.BlockSpec(memory_space=pl.ANY)
    vmem = pl.BlockSpec(memory_space=pltpu.VMEM)
    dma = pltpu.SemaphoreType.DMA
    student_all, error_term, grad_gain, loss = pl.pallas_call(
        functools.partial(body, n_row, n_col),
        out_shape=(
            jax.ShapeDtypeStruct((tokens, d_s), bf16),
            jax.ShapeDtypeStruct((tokens, width), bf16),
            jax.ShapeDtypeStruct((segments, LANES), f32),
            jax.ShapeDtypeStruct((1, LANES), f32),
        ),
        in_specs=[anywhere, anywhere, anywhere, vmem, anywhere, vmem, anywhere],
        out_specs=(anywhere, anywhere, vmem, vmem),
        scratch_shapes=[
            pltpu.VMEM((tokens, d_s), bf16),
            pltpu.VMEM((tokens, width), bf16),
            pltpu.VMEM((tokens, context.shape[1]), bf16),
            pltpu.VMEM(out_weight.shape, bf16),
            pltpu.VMEM((d_s, width), bf16),
            pltpu.VMEM((n_col, tokens, width), f32),
            pltpu.VMEM((n_col - 1, tokens, width), bf16),
            pltpu.VMEM((n_col, tokens, width), bf16),
            pltpu.VMEM((tokens, width), bf16),
            pltpu.VMEM((devices,) + student_hidden.shape, bf16),
            pltpu.VMEM((tokens, d_s), f32),
            pltpu.VMEM((1, d_s), f32),
            pltpu.VMEM((1, width), f32),
            pltpu.VMEM((tokens, width), f32),
            pltpu.VMEM((tokens, width), f32),
            pltpu.VMEM((1, tokens), f32),
            pltpu.VMEM((devices, 1, tokens), f32),
            pltpu.VMEM((d_s // LANES, 2, LANES), f32),
            pltpu.VMEM((devices, 2, LANES), f32),
            pltpu.VMEM((1, LANES), f32),
            pltpu.VMEM((devices, 1, LANES), f32),
            dma((6,)),
            dma((CHUNKS,)),
            dma((3, chips, CHUNKS)),
            dma((n_row, CHUNKS)),
            dma((3, chips)),
            dma((n_col, chips)),
            dma((n_col, chips)),
            dma((devices,)),
            dma((2, n_col)),
            dma((2, n_col)),
            dma((3,)),
            dma((3,)),
        ],
        compiler_params=pltpu.CompilerParams(
            collective_id=0, has_side_effects=True, vmem_limit_bytes=67_000_000
        ),
    )(
        context, out_weight, residual, teacher_gain.reshape(-1, LANES), student_hidden,
        student_gain.reshape(-1, LANES), projector,
    )
    grad_proj, grad_gain, loss = project_call(student_all, error_term, grad_gain, loss)
    return (grad_proj, grad_gain.reshape(-1), loss[0, 0])


def solution(mesh):
    placed = (
        P("row", "col"),
        P("col", "row"),
        P("col", "row"),
        P(),
        P(("row", "col"), None),
        P(),
        P(None, ("row", "col")),
    )
    return jax.shard_map(
        functools.partial(per_device, mesh.shape["row"], mesh.shape["col"]),
        mesh=mesh,
        in_specs=placed,
        out_specs=(P(None, ("row", "col")), P(), P()),
        check_vma=False,
    )
```

```python
import functools

import jax
import jax.numpy as jnp
from jax import lax
from jax.experimental import pallas as pl
from jax.experimental.pallas import tpu as pltpu
from jax.sharding import PartitionSpec as P

norm_eps = 1e-05
LANES = 128
CHUNKS = 2
DIRECT = 2
MESH = pl.DeviceIdType.MESH


def body(
    n_row, n_col,
    context, weight, residual, teacher_gain, hidden, student_gain, projector,
    student_out, error_out, gain_out, loss_out,
    student, error, ctx, w, proj, tail_acc, own_part, part_out, part_in, res, hid, normed, sgain, tgain,
    predicted, total, both, squares, sq_out, sq_in, fixed, gp, gp_in, gs, gs_in, final,
    local_sem, w_sem, ctx_send, ctx_fwd, ctx_side, ctx_recv, hid_z, hid_side, hid_pair, hid_recv, hid_row,
    col_send, col_recv, all_send, all_recv, pair_send, pair_recv,
):
    devices = n_row * n_col
    chips = n_row // 2
    r, c = lax.axis_index("row"), lax.axis_index("col")
    me = r * n_col + c
    p, core = r // 2, r % 2
    tok, features = context.shape
    chunk = features // CHUNKS
    tokens = tok * n_row
    width = proj.shape[1]
    res_rows = residual.shape[0]
    hid_rows, d_s = hidden.shape
    d_t = width * devices
    f32, bf16 = jnp.float32, jnp.bfloat16
    partner = (r + 1 - 2 * core, c)

    far = max(1, chips // 4)
    low = p < chips // 2
    group = 2 * tok
    tail_rows, main_rows = far * group, (chips - far) * group
    tail_first = jnp.where(low, chips - far, 0)
    main_first = jnp.where(low, 0, far)
    tail_at = pl.ds(pl.multiple_of(tail_first * group, group), tail_rows)
    main_at = pl.ds(pl.multiple_of(main_first * group, group), main_rows)

    def peer(i):
        return (c + 1 + i) % n_col

    def same_core(i):
        return ((p + 1 + i) % chips) * 2 + core

    def remote(src, dst, send_sem, recv_sem, device):
        return pltpu.make_async_remote_copy(
            src_ref=src, dst_ref=dst, send_sem=send_sem, recv_sem=recv_sem,
            device_id=device, device_id_type=MESH,
        )

    def done(ref, sem):
        pltpu.make_async_copy(ref, ref, sem).wait()

    barrier = pltpu.get_barrier_semaphore()

    def greet(device):
        pl.semaphore_signal(barrier, inc=1, device_id=device, device_id_type=MESH)

    greet(partner)
    for i in range(chips - 1):
        greet((same_core(i), c))
    for i in range(n_col - 1):
        greet((r, peer(i)))

    def rows_of(row):
        return pl.ds(pl.multiple_of(row * tok, tok), tok)

    def cols_of(k):
        return pl.ds(k * chunk, chunk)

    def res_place(j):
        return res.at[pl.ds(pl.multiple_of(j * res_rows, res_rows), res_rows), :]

    def res_part(j):
        return residual.at[:, pl.ds(pl.multiple_of(j * width, width), width)]

    ctx_copy = pltpu.make_async_copy(context, ctx.at[rows_of(r), :], local_sem.at[0])
    hid_copy = pltpu.make_async_copy(hidden, hid.at[me], local_sem.at[1])
    res_copy = pltpu.make_async_copy(res_part(c), res_place(c), local_sem.at[2])
    proj_copy = pltpu.make_async_copy(projector, proj, local_sem.at[3])
    ctx_copy.start()
    hid_copy.start()

    def w_copy(k):
        part = pl.ds(k * chunk, chunk)
        return pltpu.make_async_copy(weight.at[part, :], w.at[part, :], w_sem.at[k])

    for k in range(CHUNKS):
        w_copy(k).start()
    res_copy.start()
    proj_copy.start()
    pl.semaphore_wait(barrier, 1 + chips - 1 + n_col - 1)

    def inside(pos):
        return (pos >= 0) & (pos < chips)

    def block(pos, k):
        return ctx.at[rows_of(pos * 2 + core), cols_of(k)]

    def ctx_direct(way, d, k):
        sign = 1 - 2 * way
        return remote(
            context.at[:, cols_of(k)], block(p, k), ctx_send.at[way, d - 1, k], ctx_recv.at[r, k],
            ((p + sign * d) * 2 + core, c),
        )

    def ctx_onward(way, pos, k):
        sign = 1 - 2 * way
        return remote(
            block(pos, k), block(pos, k), ctx_fwd.at[way, pos, k], ctx_recv.at[pos * 2 + core, k],
            ((p + sign) * 2 + core, c),
        )

    def ctx_across(pos, k, first=False):
        src = context.at[:, cols_of(k)] if first else block(pos, k)
        return remote(src, block(pos, k), ctx_side.at[pos, k], ctx_recv.at[pos * 2 + core, k], partner)

    for d in range(min(DIRECT, chips - 1), 0, -1):
        for k in range(CHUNKS):
            for way in range(2):
                @pl.when(inside(p + (1 - 2 * way) * d))
                def _(way=way, d=d, k=k):
                    ctx_direct(way, d, k).start()
    for k in range(CHUNKS):
        ctx_across(p, k, True).start()

    def slot(pos, col):
        return hid.at[(pos * 2 + core) * n_col + col]

    def row_slots(row):
        return hid.at[pl.ds(pl.multiple_of(row * n_col, n_col), n_col)]

    def hid_to_z(i):
        return remote(hidden, slot(p, c), hid_z.at[i], hid_recv.at[p, c], (same_core(i), c))

    def hid_to_side(pos, i, first=False):
        src = hidden if first else slot(pos, c)
        return remote(src, slot(pos, c), hid_side.at[i, pos], hid_recv.at[pos, c], (r, peer(i)))

    def hid_to_pair(pos):
        row = pos * 2 + core
        return remote(row_slots(row), row_slots(row), hid_pair.at[pos], hid_row.at[pos], partner)

    def res_send(i):
        return remote(res_part(peer(i)), res_place(c), col_send.at[0, i], col_recv.at[0, c], (r, peer(i)))

    for i in range(chips - 1):
        hid_to_z(i).start()
    for i in range(n_col - 1):
        hid_to_side(p, i, True).start()
        res_send(i).start()

    def arrive(d, k):
        for way in range(2):
            sign = 1 - 2 * way
            pos = p - sign * d

            @pl.when(inside(pos))
            def _(way=way, sign=sign, pos=pos):
                done(block(pos, k), ctx_recv.at[pos * 2 + core, k])
                if d >= DIRECT:
                    @pl.when(inside(p + sign))
                    def _():
                        ctx_onward(way, pos, k).start()
                ctx_across(pos, k).start()

    for k in range(CHUNKS):
        arrive(DIRECT, k)
    for d in range(1, DIRECT):
        for k in range(CHUNKS):
            arrive(d, k)

    def from_partner(pos, k):
        row = pos * 2 + 1 - core
        done(ctx.at[rows_of(row), cols_of(k)], ctx_recv.at[row, k])

    def part_send(stage, i, at):
        return remote(
            part_out.at[i, at, :], part_in.at[c, at, :], col_send.at[1 + stage, i],
            col_recv.at[1 + stage, c], (r, peer(i)),
        )

    def product(at, j, first, count):
        rows = slice(first * chunk, (first + count) * chunk)
        cols = pl.ds(pl.multiple_of(j * width, width), width)
        return jnp.dot(ctx[at, rows], w[rows, cols], preferred_element_type=f32)

    for d in range(DIRECT + 1, chips - far):
        for k in range(CHUNKS):
            arrive(d, k)
    ctx_copy.wait()
    for k in range(CHUNKS):
        for i in range(chips - far):
            from_partner(main_first + i, k)
        w_copy(k).wait()
    for i in range(n_col - 1):
        part_out[i, main_at, :] = product(main_at, peer(i), 0, CHUNKS).astype(bf16)
        part_send(0, i, main_at).start()
    own_part[main_at, :] = product(main_at, c, 0, CHUNKS)

    for i in range(chips - 1):
        pos = (p + 1 + i) % chips
        done(slot(pos, c), hid_recv.at[pos, c])
        for q in range(n_col - 1):
            hid_to_side(pos, q).start()

    for k in range(CHUNKS):
        for d in range(max(DIRECT + 1, chips - far), chips):
            arrive(d, k)
        for i in range(far):
            from_partner(tail_first + i, k)
        for i in range(n_col):
            j = peer(i)
            part = product(tail_at, j, k, 1)
            if k > 0:
                part = part + tail_acc[i]
            if k < CHUNKS - 1:
                tail_acc[i] = part
            elif i < n_col - 1:
                part_out[i, tail_at, :] = part.astype(bf16)
                part_send(1, i, tail_at).start()
            else:
                own_part[tail_at, :] = part

    hid_copy.wait()
    for i in range(chips):
        pos = (p + i) % chips
        for q in range(n_col - 1):
            j = peer(q)
            done(slot(pos, j), hid_recv.at[pos, j])
        hid_to_pair(pos).start()

    for j in range(student_gain.shape[0]):
        sgain[:, j * LANES:(j + 1) * LANES] = student_gain[j:j + 1, :]
    gain_rows = width // LANES
    for j in range(gain_rows):
        tgain[:, j * LANES:(j + 1) * LANES] = teacher_gain[pl.ds(me * gain_rows + j, 1), :]

    res_copy.wait()
    for i in range(n_col - 1):
        j = peer(i)
        done(res_place(j), col_recv.at[0, j])

    def gather_parts(stage, at, rows):
        for i in range(n_col - 1):
            j = peer(i)
            done(part_in.at[j, at, :], col_recv.at[1 + stage, j])
        summed = own_part[at, :] + res[at, :].astype(f32)
        for i in range(n_col - 1):
            summed = summed + part_in[peer(i), at, :].astype(f32)
        total[at, :] = summed
        squares[at, :] = jnp.broadcast_to(jnp.sum(summed * summed, axis=1, keepdims=True), (rows, LANES))

    gather_parts(0, main_at, main_rows)

    for i in range(chips):
        pos = (p + i) % chips
        done(row_slots(pos * 2 + 1 - core), hid_row.at[pos])

    tile = 16
    eight = 8 // hid_rows if hid_rows < 8 else 1
    per = tile // hid_rows

    def normalize(t, _):
        at = pl.ds(pl.multiple_of(t * tile, tile), tile)
        x = jnp.concatenate(
            [
                jnp.concatenate([hid[t * per + g + i].astype(f32) for i in range(eight)], axis=0)
                for g in range(0, per, eight)
            ],
            axis=0,
        )
        x = x * lax.rsqrt(jnp.mean(x * x, axis=1, keepdims=True) + norm_eps)
        normed[at, :] = x
        student[at, :] = (x * sgain[...]).astype(bf16)
        return 0

    lax.fori_loop(0, tokens // tile, normalize, 0)
    student_copy = pltpu.make_async_copy(student, student_out, local_sem.at[4])
    student_copy.start()

    gather_parts(1, tail_at, tail_rows)
    for b in range(tokens // LANES):
        lanes = slice(b * LANES, (b + 1) * LANES)
        row = jnp.transpose(squares[lanes, :])[0:1, :]
        sq_out[:, lanes] = row
        sq_in[me, :, lanes] = row

    def send_sq(i, _):
        d = (me + 1 + i) % devices
        remote(sq_out, sq_in.at[me], all_send.at[0], all_recv.at[0], (d // n_col, d % n_col)).start()
        return 0

    lax.fori_loop(0, devices - 1, send_sq, 0)

    proj_copy.wait()
    predicted[...] = jnp.dot(student[...], proj[...], preferred_element_type=f32)
    both[0:tokens, :] = predicted[...].astype(bf16)
    both[tokens:, :] = (total[...] * tgain[...]).astype(bf16)
    step = 512

    def early(n, _):
        at = pl.ds(pl.multiple_of(n * step, step), step)
        back = lax.dot_general(
            both[...], proj[at, :], (((1,), (1,)), ((), ())), preferred_element_type=f32
        )
        x = normed[:, at]
        fixed[:, at] = jnp.sum(back[0:tokens, :] * x, axis=0, keepdims=True)
        normed[:, at] = back[tokens:, :] * x
        return 0

    lax.fori_loop(0, d_s // step, early, 0)

    others = sq_in.at[pl.ds(0, devices - 1)]
    done(others, all_recv.at[0])
    factor = lax.rsqrt(jnp.sum(sq_in[...], axis=0) / d_t + norm_eps)
    blocks = [slice(b * LANES, (b + 1) * LANES) for b in range(tokens // LANES)]
    scales = [jnp.transpose(jnp.broadcast_to(factor[:, lanes], (LANES, LANES))) for lanes in blocks]
    half = d_s // LANES // 2
    for q in range(2 * half):
        lanes = slice(q * LANES, (q + 1) * LANES)
        moved = jnp.zeros((1, LANES), f32)
        for at, scale in zip(blocks, scales):
            moved = moved + jnp.sum(normed[at, lanes] * scale, axis=0, keepdims=True)
        gp[q // half, q % half:q % half + 1, :] = (fixed[:, lanes] - moved) * (1.0 / 64.0)
    loss_part = jnp.zeros((1, 1), f32)
    for at, scale in zip(blocks, scales):
        target = (total[at, :] * scale[:, 0:1] * tgain[...]).astype(bf16)
        difference = predicted[at, :] - target.astype(f32)
        loss_part = loss_part + jnp.sum(difference * difference, keepdims=True)
        error[at, :] = (difference * (1.0 / 64.0)).astype(bf16)
    loss_row = jnp.broadcast_to(loss_part, (1, LANES))
    gp[0, half:half + 1, :] = loss_row
    gp[1, half:half + 1, :] = loss_row

    give = remote(gp.at[1 - core], gp_in, pair_send.at[0], pair_recv.at[0], partner)
    give.start()
    error_copy = pltpu.make_async_copy(error, error_out, local_sem.at[5])
    error_copy.start()
    give.wait_recv()
    place = p * n_col + c
    gs[...] = gp[core] + gp_in[...]
    gs_in[place] = gs[...]
    count = chips * n_col

    def send_gain(i, _):
        d = (place + 1 + i) % count
        remote(
            gs, gs_in.at[place], all_send.at[1], all_recv.at[1], ((d // n_col) * 2 + core, d % n_col)
        ).start()
        return 0

    lax.fori_loop(0, count - 1, send_gain, 0)
    rest = gs_in.at[pl.ds(0, count - 1)]

    student_copy.wait()
    error_copy.wait()
    for k in range(CHUNKS):
        for way in range(2):
            sign = 1 - 2 * way
            for d in range(1, min(DIRECT, chips - 1) + 1):
                @pl.when(inside(p + sign * d))
                def _(way=way, d=d, k=k):
                    done(context.at[:, cols_of(k)], ctx_send.at[way, d - 1, k])
            for d in range(DIRECT, chips):
                pos = p - sign * d

                @pl.when(inside(pos) & inside(p + sign))
                def _(way=way, pos=pos, k=k):
                    done(block(pos, k), ctx_fwd.at[way, pos, k])
        for pos in range(chips):
            done(block(pos, k), ctx_side.at[pos, k])
    for i in range(chips - 1):
        done(hidden, hid_z.at[i])
    for i in range(n_col - 1):
        for pos in range(chips):
            done(slot(pos, c), hid_side.at[i, pos])
        done(res_part(peer(i)), col_send.at[0, i])
        done(part_out.at[i, main_at, :], col_send.at[1, i])
        done(part_out.at[i, tail_at, :], col_send.at[2, i])
    for pos in range(chips):
        done(row_slots(pos * 2 + core), hid_pair.at[pos])
    done(others, all_send.at[0])
    give.wait_send()

    done(rest, all_recv.at[1])
    final[core] = jnp.sum(gs_in[...], axis=0)
    swap = remote(final.at[core], final.at[core], pair_send.at[1], pair_recv.at[1], partner)
    swap.start()
    done(rest, all_send.at[1])
    loss_out[...] = final[core, half:half + 1, :] / (tokens * d_t)
    done(final.at[1 - core], pair_recv.at[1])
    gain_out[0:half, :] = final[0, 0:half, :]
    gain_out[half:, :] = final[1, 0:half, :]
    swap.wait_send()


def project(student_in, error_in, gain_in, loss_in, grad_out, gain_out, loss_out,
            student, error, grad, in_sem, out_sem):
    n, _, step = student.shape
    error_copy = pltpu.make_async_copy(error_in, error, in_sem.at[n])
    error_copy.start()

    def fetch(i):
        cols = pl.ds(pl.multiple_of(i * step, step), step)
        return pltpu.make_async_copy(student_in.at[:, cols], student.at[i], in_sem.at[i])

    def write(i):
        rows = pl.ds(pl.multiple_of(i * step, step), step)
        return pltpu.make_async_copy(grad.at[i], grad_out.at[rows, :], out_sem.at[i])

    for i in range(n):
        fetch(i).start()
    small = [
        pltpu.make_async_copy(gain_in, gain_out, in_sem.at[n + 1]),
        pltpu.make_async_copy(loss_in, loss_out, in_sem.at[n + 2]),
    ]
    for copy in small:
        copy.start()
    error_copy.wait()

    def block(i, _):
        fetch(i).wait()
        grad[i] = lax.dot_general(
            student[i], error[...], (((0,), (0,)), ((), ())), preferred_element_type=jnp.float32
        )
        write(i).start()
        return 0

    lax.fori_loop(0, n, block, 0)
    for i in range(n):
        write(i).wait()
    for copy in small:
        copy.wait()


def project_call(student_all, error_term, gain, loss):
    tokens, d_s = student_all.shape
    width = error_term.shape[1]
    steps = 8
    rows = d_s // steps
    hbm = pl.BlockSpec(memory_space=pltpu.HBM)
    f32, bf16 = jnp.float32, jnp.bfloat16
    return pl.pallas_call(
        project,
        out_shape=(
            jax.ShapeDtypeStruct((d_s, width), f32),
            jax.ShapeDtypeStruct(gain.shape, f32),
            jax.ShapeDtypeStruct(loss.shape, f32),
        ),
        in_specs=[hbm] * 4,
        out_specs=(hbm,) * 3,
        scratch_shapes=[
            pltpu.VMEM((steps, tokens, rows), bf16),
            pltpu.VMEM((tokens, width), bf16),
            pltpu.VMEM((steps, rows, width), f32),
            pltpu.SemaphoreType.DMA((steps + 3,)),
            pltpu.SemaphoreType.DMA((steps,)),
        ],
        compiler_params=pltpu.CompilerParams(vmem_limit_bytes=67_000_000),
    )(student_all, error_term, gain, loss)


def per_device(
    n_row, n_col,
    context, out_weight, residual, teacher_gain, student_hidden, student_gain, projector,
):
    devices = n_row * n_col
    chips = n_row // 2
    tokens = context.shape[0] * n_row
    d_s, width = projector.shape
    half = d_s // LANES // 2
    f32, bf16 = jnp.float32, jnp.bfloat16
    anywhere = pl.BlockSpec(memory_space=pl.ANY)
    vmem = pl.BlockSpec(memory_space=pltpu.VMEM)
    dma = pltpu.SemaphoreType.DMA
    student_all, error_term, grad_gain, loss = pl.pallas_call(
        functools.partial(body, n_row, n_col),
        out_shape=(
            jax.ShapeDtypeStruct((tokens, d_s), bf16),
            jax.ShapeDtypeStruct((tokens, width), bf16),
            jax.ShapeDtypeStruct((2 * half, LANES), f32),
            jax.ShapeDtypeStruct((1, LANES), f32),
        ),
        in_specs=[anywhere, anywhere, anywhere, vmem, anywhere, vmem, anywhere],
        out_specs=(anywhere, anywhere, vmem, vmem),
        scratch_shapes=[
            pltpu.VMEM((tokens, d_s), bf16),
            pltpu.VMEM((tokens, width), bf16),
            pltpu.VMEM((tokens, context.shape[1]), bf16),
            pltpu.VMEM(out_weight.shape, bf16),
            pltpu.VMEM((d_s, width), bf16),
            pltpu.VMEM((n_col, max(1, chips // 4) * 2 * context.shape[0], width), f32),
            pltpu.VMEM((tokens, width), f32),
            pltpu.VMEM((n_col - 1, tokens, width), bf16),
            pltpu.VMEM((n_col, tokens, width), bf16),
            pltpu.VMEM((tokens, width), bf16),
            pltpu.VMEM((devices,) + student_hidden.shape, bf16),
            pltpu.VMEM((tokens, d_s), f32),
            pltpu.VMEM((1, d_s), f32),
            pltpu.VMEM((1, width), f32),
            pltpu.VMEM((tokens, width), f32),
            pltpu.VMEM((tokens, width), f32),
            pltpu.VMEM((2 * tokens, width), bf16),
            pltpu.VMEM((tokens, LANES), f32),
            pltpu.VMEM((1, tokens), f32),
            pltpu.VMEM((devices, 1, tokens), f32),
            pltpu.VMEM((1, d_s), f32),
            pltpu.VMEM((2, half + 1, LANES), f32),
            pltpu.VMEM((half + 1, LANES), f32),
            pltpu.VMEM((half + 1, LANES), f32),
            pltpu.VMEM((chips * n_col, half + 1, LANES), f32),
            pltpu.VMEM((2, half + 1, LANES), f32),
            dma((6,)),
            dma((CHUNKS,)),
            dma((2, DIRECT, CHUNKS)),
            dma((2, chips, CHUNKS)),
            dma((chips, CHUNKS)),
            dma((n_row, CHUNKS)),
            dma((chips,)),
            dma((n_col, chips)),
            dma((chips,)),
            dma((chips, n_col)),
            dma((chips,)),
            dma((3, n_col)),
            dma((3, n_col)),
            dma((2,)),
            dma((2,)),
            dma((2,)),
            dma((2,)),
        ],
        compiler_params=pltpu.CompilerParams(
            collective_id=0, has_side_effects=True, vmem_limit_bytes=67_000_000
        ),
    )(
        context, out_weight, residual, teacher_gain.reshape(-1, LANES), student_hidden,
        student_gain.reshape(-1, LANES), projector,
    )
    grad_proj, grad_gain, loss = project_call(student_all, error_term, grad_gain, loss)
    return (grad_proj, grad_gain.reshape(-1), loss[0, 0])


def solution(mesh):
    placed = (
        P("row", "col"),
        P("col", "row"),
        P("col", "row"),
        P(),
        P(("row", "col"), None),
        P(),
        P(None, ("row", "col")),
    )
    return jax.shard_map(
        functools.partial(per_device, mesh.shape["row"], mesh.shape["col"]),
        mesh=mesh,
        in_specs=placed,
        out_specs=(P(None, ("row", "col")), P(), P()),
        check_vma=False,
    )
```

```python
import functools

import jax
import jax.numpy as jnp
from jax import lax
from jax.experimental import pallas as pl
from jax.experimental.pallas import tpu as pltpu
from jax.sharding import PartitionSpec as P

norm_eps = 1e-05
LANES = 128
CHUNKS = 2
DIRECT = 2
STORES = 8
MESH = pl.DeviceIdType.MESH


def body(
    n_row, n_col,
    context, weight, residual, teacher_gain, hidden, student_gain, projector,
    grad_out, gain_out, loss_out,
    student, error, ctx, w, proj, tail_acc, own_part, part_out, part_in, res, hid, normed, sgain, tgain,
    predicted, total, both, squares, sq_out, sq_in, fixed, gp, gp_in, gs, gs_in, final,
    local_sem, w_sem, ctx_send, ctx_fwd, ctx_side, ctx_recv, hid_z, hid_side, hid_pair, hid_recv, hid_row,
    col_send, col_recv, all_send, all_recv, pair_send, pair_recv,
):
    devices = n_row * n_col
    chips = n_row // 2
    r, c = lax.axis_index("row"), lax.axis_index("col")
    me = r * n_col + c
    p, core = r // 2, r % 2
    tok, features = context.shape
    chunk = features // CHUNKS
    tokens = tok * n_row
    width = proj.shape[1]
    res_rows = residual.shape[0]
    hid_rows, d_s = hidden.shape
    d_t = width * devices
    f32, bf16 = jnp.float32, jnp.bfloat16
    partner = (r + 1 - 2 * core, c)

    far = max(1, chips // 4)
    low = p < chips // 2
    group = 2 * tok
    tail_rows, main_rows = far * group, (chips - far) * group
    tail_first = jnp.where(low, chips - far, 0)
    main_first = jnp.where(low, 0, far)
    tail_at = pl.ds(pl.multiple_of(tail_first * group, group), tail_rows)
    main_at = pl.ds(pl.multiple_of(main_first * group, group), main_rows)

    def peer(i):
        return (c + 1 + i) % n_col

    def same_core(i):
        return ((p + 1 + i) % chips) * 2 + core

    def remote(src, dst, send_sem, recv_sem, device):
        return pltpu.make_async_remote_copy(
            src_ref=src, dst_ref=dst, send_sem=send_sem, recv_sem=recv_sem,
            device_id=device, device_id_type=MESH,
        )

    def done(ref, sem):
        pltpu.make_async_copy(ref, ref, sem).wait()

    barrier = pltpu.get_barrier_semaphore()

    def greet(device):
        pl.semaphore_signal(barrier, inc=1, device_id=device, device_id_type=MESH)

    greet(partner)
    for i in range(chips - 1):
        greet((same_core(i), c))
    for i in range(n_col - 1):
        greet((r, peer(i)))

    def rows_of(row):
        return pl.ds(pl.multiple_of(row * tok, tok), tok)

    def cols_of(k):
        return pl.ds(k * chunk, chunk)

    def res_place(j):
        return res.at[pl.ds(pl.multiple_of(j * res_rows, res_rows), res_rows), :]

    def res_part(j):
        return residual.at[:, pl.ds(pl.multiple_of(j * width, width), width)]

    ctx_copy = pltpu.make_async_copy(context, ctx.at[rows_of(r), :], local_sem.at[0])
    hid_copy = pltpu.make_async_copy(hidden, hid.at[me], local_sem.at[1])
    res_copy = pltpu.make_async_copy(res_part(c), res_place(c), local_sem.at[2])
    proj_copy = pltpu.make_async_copy(projector, proj, local_sem.at[3])
    ctx_copy.start()
    hid_copy.start()

    def w_copy(k):
        part = pl.ds(k * chunk, chunk)
        return pltpu.make_async_copy(weight.at[part, :], w.at[part, :], w_sem.at[k])

    for k in range(CHUNKS):
        w_copy(k).start()
    res_copy.start()
    proj_copy.start()
    pl.semaphore_wait(barrier, 1 + chips - 1 + n_col - 1)

    def inside(pos):
        return (pos >= 0) & (pos < chips)

    def block(pos, k):
        return ctx.at[rows_of(pos * 2 + core), cols_of(k)]

    def ctx_direct(way, d, k):
        sign = 1 - 2 * way
        return remote(
            context.at[:, cols_of(k)], block(p, k), ctx_send.at[way, d - 1, k], ctx_recv.at[r, k],
            ((p + sign * d) * 2 + core, c),
        )

    def ctx_onward(way, pos, k):
        sign = 1 - 2 * way
        return remote(
            block(pos, k), block(pos, k), ctx_fwd.at[way, pos, k], ctx_recv.at[pos * 2 + core, k],
            ((p + sign) * 2 + core, c),
        )

    def ctx_across(pos, k, first=False):
        src = context.at[:, cols_of(k)] if first else block(pos, k)
        return remote(src, block(pos, k), ctx_side.at[pos, k], ctx_recv.at[pos * 2 + core, k], partner)

    def slot(pos, col):
        return hid.at[(pos * 2 + core) * n_col + col]

    def row_slots(row):
        return hid.at[pl.ds(pl.multiple_of(row * n_col, n_col), n_col)]

    def hid_to_z(i):
        return remote(hidden, slot(p, c), hid_z.at[i], hid_recv.at[p, c], (same_core(i), c))

    def hid_to_side(pos, i, first=False):
        src = hidden if first else slot(pos, c)
        return remote(src, slot(pos, c), hid_side.at[i, pos], hid_recv.at[pos, c], (r, peer(i)))

    def hid_to_pair(pos):
        row = pos * 2 + core
        return remote(row_slots(row), row_slots(row), hid_pair.at[pos], hid_row.at[pos], partner)

    def res_send(i):
        return remote(res_part(peer(i)), res_place(c), col_send.at[0, i], col_recv.at[0, c], (r, peer(i)))

    for i in range(chips - 1):
        hid_to_z(i).start()
    for i in range(n_col - 1):
        hid_to_side(p, i, True).start()
    for d in range(min(DIRECT, chips - 1), 0, -1):
        for k in range(CHUNKS):
            for way in range(2):
                @pl.when(inside(p + (1 - 2 * way) * d))
                def _(way=way, d=d, k=k):
                    ctx_direct(way, d, k).start()
    for k in range(CHUNKS):
        ctx_across(p, k, True).start()

    def arrive(d, k):
        for way in range(2):
            sign = 1 - 2 * way
            pos = p - sign * d

            @pl.when(inside(pos))
            def _(way=way, sign=sign, pos=pos):
                done(block(pos, k), ctx_recv.at[pos * 2 + core, k])
                if d >= DIRECT:
                    @pl.when(inside(p + sign))
                    def _():
                        ctx_onward(way, pos, k).start()
                ctx_across(pos, k).start()

    for i in range(chips - 1):
        pos = (p + 1 + i) % chips
        done(slot(pos, c), hid_recv.at[pos, c])
        for q in range(n_col - 1):
            hid_to_side(pos, q).start()

    for i in range(n_col - 1):
        res_send(i).start()
    for k in range(CHUNKS):
        arrive(DIRECT, k)
    for d in range(1, DIRECT):
        for k in range(CHUNKS):
            arrive(d, k)

    def from_partner(pos, k):
        row = pos * 2 + 1 - core
        done(ctx.at[rows_of(row), cols_of(k)], ctx_recv.at[row, k])

    def part_send(stage, i, at):
        return remote(
            part_out.at[i, at, :], part_in.at[c, at, :], col_send.at[1 + stage, i],
            col_recv.at[1 + stage, c], (r, peer(i)),
        )

    def product(at, j, first, count):
        rows = slice(first * chunk, (first + count) * chunk)
        cols = pl.ds(pl.multiple_of(j * width, width), width)
        return jnp.dot(ctx[at, rows], w[rows, cols], preferred_element_type=f32)

    for d in range(DIRECT + 1, chips - far):
        for k in range(CHUNKS):
            arrive(d, k)
    ctx_copy.wait()
    for k in range(CHUNKS):
        for i in range(chips - far):
            from_partner(main_first + i, k)
        w_copy(k).wait()
    for i in range(n_col - 1):
        part_out[i, main_at, :] = product(main_at, peer(i), 0, CHUNKS).astype(bf16)
        part_send(0, i, main_at).start()
    own_part[main_at, :] = product(main_at, c, 0, CHUNKS)

    hid_copy.wait()
    for i in range(chips):
        pos = (p + i) % chips
        for q in range(n_col - 1):
            j = peer(q)
            done(slot(pos, j), hid_recv.at[pos, j])
        hid_to_pair(pos).start()

    for k in range(CHUNKS):
        for d in range(max(DIRECT + 1, chips - far), chips):
            arrive(d, k)
        for i in range(far):
            from_partner(tail_first + i, k)
        for i in range(n_col):
            j = peer(i)
            part = product(tail_at, j, k, 1)
            if k > 0:
                part = part + tail_acc[i]
            if k < CHUNKS - 1:
                tail_acc[i] = part
            elif i < n_col - 1:
                part_out[i, tail_at, :] = part.astype(bf16)
                part_send(1, i, tail_at).start()
            else:
                own_part[tail_at, :] = part

    for j in range(student_gain.shape[0]):
        sgain[:, j * LANES:(j + 1) * LANES] = student_gain[j:j + 1, :]
    gain_rows = width // LANES
    for j in range(gain_rows):
        tgain[:, j * LANES:(j + 1) * LANES] = teacher_gain[pl.ds(me * gain_rows + j, 1), :]

    res_copy.wait()
    for i in range(n_col - 1):
        j = peer(i)
        done(res_place(j), col_recv.at[0, j])

    def gather_parts(stage, at, rows):
        for i in range(n_col - 1):
            j = peer(i)
            done(part_in.at[j, at, :], col_recv.at[1 + stage, j])
        summed = own_part[at, :] + res[at, :].astype(f32)
        for i in range(n_col - 1):
            summed = summed + part_in[peer(i), at, :].astype(f32)
        total[at, :] = summed
        squares[at, :] = jnp.broadcast_to(jnp.sum(summed * summed, axis=1, keepdims=True), (rows, LANES))

    gather_parts(0, main_at, main_rows)

    for i in range(chips):
        pos = (p + i) % chips
        done(row_slots(pos * 2 + 1 - core), hid_row.at[pos])

    tile = 16
    eight = 8 // hid_rows if hid_rows < 8 else 1
    per = tile // hid_rows

    def normalize(t, _):
        at = pl.ds(pl.multiple_of(t * tile, tile), tile)
        x = jnp.concatenate(
            [
                jnp.concatenate([hid[t * per + g + i].astype(f32) for i in range(eight)], axis=0)
                for g in range(0, per, eight)
            ],
            axis=0,
        )
        x = x * lax.rsqrt(jnp.mean(x * x, axis=1, keepdims=True) + norm_eps)
        normed[at, :] = x
        student[at, :] = (x * sgain[...]).astype(bf16)
        return 0

    lax.fori_loop(0, tokens // tile, normalize, 0)

    gather_parts(1, tail_at, tail_rows)
    for b in range(tokens // LANES):
        lanes = slice(b * LANES, (b + 1) * LANES)
        row = jnp.transpose(squares[lanes, :])[0:1, :]
        sq_out[:, lanes] = row
        sq_in[me, :, lanes] = row

    def send_sq(i, _):
        d = (me + 1 + i) % devices
        remote(sq_out, sq_in.at[me], all_send.at[0], all_recv.at[0], (d // n_col, d % n_col)).start()
        return 0

    lax.fori_loop(0, devices - 1, send_sq, 0)

    proj_copy.wait()
    predicted[...] = jnp.dot(student[...], proj[...], preferred_element_type=f32)
    both[0:tokens, :] = predicted[...].astype(bf16)
    both[tokens:, :] = (total[...] * tgain[...]).astype(bf16)
    step = 512

    def early(n, _):
        at = pl.ds(pl.multiple_of(n * step, step), step)
        back = lax.dot_general(
            both[...], proj[at, :], (((1,), (1,)), ((), ())), preferred_element_type=f32
        )
        x = normed[:, at]
        fixed[:, at] = jnp.sum(back[0:tokens, :] * x, axis=0, keepdims=True)
        normed[:, at] = back[tokens:, :] * x
        return 0

    lax.fori_loop(0, d_s // step, early, 0)

    others = sq_in.at[pl.ds(0, devices - 1)]
    done(others, all_recv.at[0])
    factor = lax.rsqrt(jnp.sum(sq_in[...], axis=0) / d_t + norm_eps)
    blocks = [slice(b * LANES, (b + 1) * LANES) for b in range(tokens // LANES)]
    scales = [jnp.transpose(jnp.broadcast_to(factor[:, lanes], (LANES, LANES))) for lanes in blocks]
    half = d_s // LANES // 2
    for q in range(2 * half):
        lanes = slice(q * LANES, (q + 1) * LANES)
        moved = jnp.zeros((1, LANES), f32)
        for at, scale in zip(blocks, scales):
            moved = moved + jnp.sum(normed[at, lanes] * scale, axis=0, keepdims=True)
        gp[q // half, q % half:q % half + 1, :] = (fixed[:, lanes] - moved) * (1.0 / 64.0)
    loss_part = jnp.zeros((1, 1), f32)
    for at, scale in zip(blocks, scales):
        target = (total[at, :] * scale[:, 0:1] * tgain[...]).astype(bf16)
        difference = predicted[at, :] - target.astype(f32)
        loss_part = loss_part + jnp.sum(difference * difference, keepdims=True)
        error[at, :] = (difference * (1.0 / 64.0)).astype(bf16)
    loss_row = jnp.broadcast_to(loss_part, (1, LANES))
    gp[0, half:half + 1, :] = loss_row
    gp[1, half:half + 1, :] = loss_row

    give = remote(gp.at[1 - core], gp_in, pair_send.at[0], pair_recv.at[0], partner)
    give.start()
    give.wait_recv()
    place = p * n_col + c
    gs[...] = gp[core] + gp_in[...]
    gs_in[place] = gs[...]
    count = chips * n_col

    def send_gain(i, _):
        d = (place + 1 + i) % count
        remote(
            gs, gs_in.at[place], all_send.at[1], all_recv.at[1], ((d // n_col) * 2 + core, d % n_col)
        ).start()
        return 0

    lax.fori_loop(0, count - 1, send_gain, 0)
    rest = gs_in.at[pl.ds(0, count - 1)]

    def project(i, _):
        at = pl.ds(pl.multiple_of(i * step, step), step)
        grad_out[at, :] = lax.dot_general(
            student[:, at], error[...], (((0,), (0,)), ((), ())), preferred_element_type=f32
        )
        return 0

    lax.fori_loop(0, d_s // step, project, 0)
    for k in range(CHUNKS):
        for way in range(2):
            sign = 1 - 2 * way
            for d in range(1, min(DIRECT, chips - 1) + 1):
                @pl.when(inside(p + sign * d))
                def _(way=way, d=d, k=k):
                    done(context.at[:, cols_of(k)], ctx_send.at[way, d - 1, k])
            for d in range(DIRECT, chips):
                pos = p - sign * d

                @pl.when(inside(pos) & inside(p + sign))
                def _(way=way, pos=pos, k=k):
                    done(block(pos, k), ctx_fwd.at[way, pos, k])
        for pos in range(chips):
            done(block(pos, k), ctx_side.at[pos, k])
    for i in range(chips - 1):
        done(hidden, hid_z.at[i])
    for i in range(n_col - 1):
        for pos in range(chips):
            done(slot(pos, c), hid_side.at[i, pos])
        done(res_part(peer(i)), col_send.at[0, i])
        done(part_out.at[i, main_at, :], col_send.at[1, i])
        done(part_out.at[i, tail_at, :], col_send.at[2, i])
    for pos in range(chips):
        done(row_slots(pos * 2 + core), hid_pair.at[pos])
    done(others, all_send.at[0])
    give.wait_send()

    done(rest, all_recv.at[1])
    final[core] = jnp.sum(gs_in[...], axis=0)
    swap = remote(final.at[core], final.at[core], pair_send.at[1], pair_recv.at[1], partner)
    swap.start()
    done(rest, all_send.at[1])
    loss_out[...] = final[core, half:half + 1, :] / (tokens * d_t)
    done(final.at[1 - core], pair_recv.at[1])
    gain_out[0:half, :] = final[0, 0:half, :]
    gain_out[half:, :] = final[1, 0:half, :]
    swap.wait_send()


def store(grad, gain_in, loss_in, grad_out, gain_out, loss_out, sem):
    steps = sem.shape[0] - 2
    size = grad.shape[0] // steps
    copies = []
    for i in range(steps):
        rows = pl.ds(i * size, size)
        copies.append(pltpu.make_async_copy(grad.at[rows, :], grad_out.at[rows, :], sem.at[i]))
    copies.append(pltpu.make_async_copy(gain_in, gain_out, sem.at[steps]))
    copies.append(pltpu.make_async_copy(loss_in, loss_out, sem.at[steps + 1]))
    for copy in copies:
        copy.start()
    for copy in copies:
        copy.wait()


def store_call(grad, gain, loss, room):
    hbm = pl.BlockSpec(memory_space=pltpu.HBM)
    return pl.pallas_call(
        store,
        out_shape=tuple(jax.ShapeDtypeStruct(a.shape, a.dtype) for a in (grad, gain, loss)),
        in_specs=[pl.BlockSpec(memory_space=pltpu.VMEM), hbm, hbm],
        out_specs=(hbm,) * 3,
        scratch_shapes=[pltpu.SemaphoreType.DMA((STORES + 2,))],
        compiler_params=pltpu.CompilerParams(vmem_limit_bytes=room),
    )(pltpu.with_memory_space_constraint(grad, pltpu.VMEM), gain, loss)


def per_device(
    n_row, n_col,
    context, out_weight, residual, teacher_gain, student_hidden, student_gain, projector,
):
    devices = n_row * n_col
    chips = n_row // 2
    tokens = context.shape[0] * n_row
    d_s, width = projector.shape
    half = d_s // LANES // 2
    f32, bf16 = jnp.float32, jnp.bfloat16
    anywhere = pl.BlockSpec(memory_space=pl.ANY)
    vmem = pl.BlockSpec(memory_space=pltpu.VMEM)
    dma = pltpu.SemaphoreType.DMA
    room = 67_000_000 - d_s * width * 4
    grad_proj, grad_gain, loss = pl.pallas_call(
        functools.partial(body, n_row, n_col),
        out_shape=(
            pltpu.VMEM((d_s, width), f32),
            jax.ShapeDtypeStruct((2 * half, LANES), f32),
            jax.ShapeDtypeStruct((1, LANES), f32),
        ),
        in_specs=[anywhere, anywhere, anywhere, vmem, anywhere, vmem, anywhere],
        out_specs=(vmem, vmem, vmem),
        scratch_shapes=[
            pltpu.VMEM((tokens, d_s), bf16),
            pltpu.VMEM((tokens, width), bf16),
            pltpu.VMEM((tokens, context.shape[1]), bf16),
            pltpu.VMEM(out_weight.shape, bf16),
            pltpu.VMEM((d_s, width), bf16),
            pltpu.VMEM((n_col, max(1, chips // 4) * 2 * context.shape[0], width), f32),
            pltpu.VMEM((tokens, width), f32),
            pltpu.VMEM((n_col - 1, tokens, width), bf16),
            pltpu.VMEM((n_col, tokens, width), bf16),
            pltpu.VMEM((tokens, width), bf16),
            pltpu.VMEM((devices,) + student_hidden.shape, bf16),
            pltpu.VMEM((tokens, d_s), f32),
            pltpu.VMEM((1, d_s), f32),
            pltpu.VMEM((1, width), f32),
            pltpu.VMEM((tokens, width), f32),
            pltpu.VMEM((tokens, width), f32),
            pltpu.VMEM((2 * tokens, width), bf16),
            pltpu.VMEM((tokens, LANES), f32),
            pltpu.VMEM((1, tokens), f32),
            pltpu.VMEM((devices, 1, tokens), f32),
            pltpu.VMEM((1, d_s), f32),
            pltpu.VMEM((2, half + 1, LANES), f32),
            pltpu.VMEM((half + 1, LANES), f32),
            pltpu.VMEM((half + 1, LANES), f32),
            pltpu.VMEM((chips * n_col, half + 1, LANES), f32),
            pltpu.VMEM((2, half + 1, LANES), f32),
            dma((6,)),
            dma((CHUNKS,)),
            dma((2, DIRECT, CHUNKS)),
            dma((2, chips, CHUNKS)),
            dma((chips, CHUNKS)),
            dma((n_row, CHUNKS)),
            dma((chips,)),
            dma((n_col, chips)),
            dma((chips,)),
            dma((chips, n_col)),
            dma((chips,)),
            dma((3, n_col)),
            dma((3, n_col)),
            dma((2,)),
            dma((2,)),
            dma((2,)),
            dma((2,)),
        ],
        compiler_params=pltpu.CompilerParams(
            collective_id=0, has_side_effects=True, vmem_limit_bytes=room
        ),
    )(
        context, out_weight, residual, teacher_gain.reshape(-1, LANES), student_hidden,
        student_gain.reshape(-1, LANES), projector,
    )
    grad_proj, grad_gain, loss = store_call(grad_proj, grad_gain, loss, room)
    return (grad_proj, grad_gain.reshape(-1), loss[0, 0])


def solution(mesh):
    placed = (
        P("row", "col"),
        P("col", "row"),
        P("col", "row"),
        P(),
        P(("row", "col"), None),
        P(),
        P(None, ("row", "col")),
    )
    return jax.shard_map(
        functools.partial(per_device, mesh.shape["row"], mesh.shape["col"]),
        mesh=mesh,
        in_specs=placed,
        out_specs=(P(None, ("row", "col")), P(), P()),
        check_vma=False,
    )
```

```python
import functools

import jax
import jax.numpy as jnp
from jax import lax
from jax.experimental import pallas as pl
from jax.experimental.pallas import tpu as pltpu
from jax.sharding import PartitionSpec as P

norm_eps = 1e-05
LANES = 128
CHUNKS = 1
DIRECT = 2
STORES = 8
MESH = pl.DeviceIdType.MESH


def body(
    n_row, n_col,
    context, weight, residual, teacher_gain, hidden, student_gain, projector,
    grad_out, gain_out, loss_out,
    student, error, ctx, w, proj, tail_acc, own_part, part_out, part_in, res, hid, normed, sgain, tgain,
    predicted, total, both, squares, sq_out, sq_in, fixed, gp, gp_in, gs, gs_in, final,
    local_sem, w_sem, ctx_send, ctx_fwd, ctx_side, ctx_recv, hid_z, hid_side, hid_pair, hid_recv, hid_row,
    col_send, col_recv, all_send, all_recv, pair_send, pair_recv,
):
    devices = n_row * n_col
    chips = n_row // 2
    r, c = lax.axis_index("row"), lax.axis_index("col")
    me = r * n_col + c
    p, core = r // 2, r % 2
    tok, features = context.shape
    chunk = features // CHUNKS
    tokens = tok * n_row
    width = proj.shape[1]
    res_rows = residual.shape[0]
    hid_rows, d_s = hidden.shape
    d_t = width * devices
    f32, bf16 = jnp.float32, jnp.bfloat16
    partner = (r + 1 - 2 * core, c)

    far = max(1, chips // 4)
    low = p < chips // 2
    group = 2 * tok
    tail_rows, main_rows = far * group, (chips - far) * group
    tail_first = jnp.where(low, chips - far, 0)
    main_first = jnp.where(low, 0, far)
    tail_at = pl.ds(pl.multiple_of(tail_first * group, group), tail_rows)
    main_at = pl.ds(pl.multiple_of(main_first * group, group), main_rows)

    def peer(i):
        return (c + 1 + i) % n_col

    def same_core(i):
        return ((p + 1 + i) % chips) * 2 + core

    def remote(src, dst, send_sem, recv_sem, device):
        return pltpu.make_async_remote_copy(
            src_ref=src, dst_ref=dst, send_sem=send_sem, recv_sem=recv_sem,
            device_id=device, device_id_type=MESH,
        )

    def done(ref, sem):
        pltpu.make_async_copy(ref, ref, sem).wait()

    barrier = pltpu.get_barrier_semaphore()

    def greet(device):
        pl.semaphore_signal(barrier, inc=1, device_id=device, device_id_type=MESH)

    greet(partner)
    for i in range(chips - 1):
        greet((same_core(i), c))
    for i in range(n_col - 1):
        greet((r, peer(i)))

    def rows_of(row):
        return pl.ds(pl.multiple_of(row * tok, tok), tok)

    def cols_of(k):
        return pl.ds(k * chunk, chunk)

    def res_place(j):
        return res.at[pl.ds(pl.multiple_of(j * res_rows, res_rows), res_rows), :]

    def res_part(j):
        return residual.at[:, pl.ds(pl.multiple_of(j * width, width), width)]

    ctx_copy = pltpu.make_async_copy(context, ctx.at[rows_of(r), :], local_sem.at[0])
    hid_copy = pltpu.make_async_copy(hidden, hid.at[me], local_sem.at[1])
    res_copy = pltpu.make_async_copy(res_part(c), res_place(c), local_sem.at[2])
    proj_copy = pltpu.make_async_copy(projector, proj, local_sem.at[3])
    ctx_copy.start()
    hid_copy.start()

    def w_copy(k):
        part = pl.ds(k * chunk, chunk)
        return pltpu.make_async_copy(weight.at[part, :], w.at[part, :], w_sem.at[k])

    for k in range(CHUNKS):
        w_copy(k).start()
    res_copy.start()
    proj_copy.start()
    pl.semaphore_wait(barrier, 1 + chips - 1 + n_col - 1)

    def inside(pos):
        return (pos >= 0) & (pos < chips)

    def block(pos, k):
        return ctx.at[rows_of(pos * 2 + core), cols_of(k)]

    def ctx_direct(way, d, k):
        sign = 1 - 2 * way
        return remote(
            context.at[:, cols_of(k)], block(p, k), ctx_send.at[way, d - 1, k], ctx_recv.at[r, k],
            ((p + sign * d) * 2 + core, c),
        )

    def ctx_onward(way, pos, k):
        sign = 1 - 2 * way
        return remote(
            block(pos, k), block(pos, k), ctx_fwd.at[way, pos, k], ctx_recv.at[pos * 2 + core, k],
            ((p + sign) * 2 + core, c),
        )

    def ctx_across(pos, k, first=False):
        src = context.at[:, cols_of(k)] if first else block(pos, k)
        return remote(src, block(pos, k), ctx_side.at[pos, k], ctx_recv.at[pos * 2 + core, k], partner)

    def slot(pos, col):
        return hid.at[(pos * 2 + core) * n_col + col]

    def row_slots(row):
        return hid.at[pl.ds(pl.multiple_of(row * n_col, n_col), n_col)]

    def hid_to_z(i):
        return remote(hidden, slot(p, c), hid_z.at[i], hid_recv.at[p, c], (same_core(i), c))

    def hid_to_side(pos, i, first=False):
        src = hidden if first else slot(pos, c)
        return remote(src, slot(pos, c), hid_side.at[i, pos], hid_recv.at[pos, c], (r, peer(i)))

    def hid_to_pair(pos):
        row = pos * 2 + core
        return remote(row_slots(row), row_slots(row), hid_pair.at[pos], hid_row.at[pos], partner)

    def res_send(i):
        return remote(res_part(peer(i)), res_place(c), col_send.at[0, i], col_recv.at[0, c], (r, peer(i)))

    for i in range(chips - 1):
        hid_to_z(i).start()
    for i in range(n_col - 1):
        hid_to_side(p, i, True).start()
    for d in range(min(DIRECT, chips - 1), 0, -1):
        for k in range(CHUNKS):
            for way in range(2):
                @pl.when(inside(p + (1 - 2 * way) * d))
                def _(way=way, d=d, k=k):
                    ctx_direct(way, d, k).start()
    for k in range(CHUNKS):
        ctx_across(p, k, True).start()

    def arrive(d, k):
        for way in range(2):
            sign = 1 - 2 * way
            pos = p - sign * d

            @pl.when(inside(pos))
            def _(way=way, sign=sign, pos=pos):
                done(block(pos, k), ctx_recv.at[pos * 2 + core, k])
                if d >= DIRECT:
                    @pl.when(inside(p + sign))
                    def _():
                        ctx_onward(way, pos, k).start()
                ctx_across(pos, k).start()

    for i in range(chips - 1):
        pos = (p + 1 + i) % chips
        done(slot(pos, c), hid_recv.at[pos, c])
        for q in range(n_col - 1):
            hid_to_side(pos, q).start()

    for i in range(n_col - 1):
        res_send(i).start()
    for k in range(CHUNKS):
        arrive(DIRECT, k)
    for d in range(1, DIRECT):
        for k in range(CHUNKS):
            arrive(d, k)

    def from_partner(pos, k):
        row = pos * 2 + 1 - core
        done(ctx.at[rows_of(row), cols_of(k)], ctx_recv.at[row, k])

    def part_send(stage, i, at):
        return remote(
            part_out.at[i, at, :], part_in.at[c, at, :], col_send.at[1 + stage, i],
            col_recv.at[1 + stage, c], (r, peer(i)),
        )

    def product(at, j, first, count):
        rows = slice(first * chunk, (first + count) * chunk)
        cols = pl.ds(pl.multiple_of(j * width, width), width)
        return jnp.dot(ctx[at, rows], w[rows, cols], preferred_element_type=f32)

    for d in range(DIRECT + 1, chips - far):
        for k in range(CHUNKS):
            arrive(d, k)
    hid_copy.wait()
    for i in range(chips):
        pos = (p + i) % chips
        for q in range(n_col - 1):
            j = peer(q)
            done(slot(pos, j), hid_recv.at[pos, j])
        hid_to_pair(pos).start()

    ctx_copy.wait()
    for k in range(CHUNKS):
        for i in range(chips - far):
            from_partner(main_first + i, k)
        w_copy(k).wait()
    for i in range(n_col - 1):
        part_out[i, main_at, :] = product(main_at, peer(i), 0, CHUNKS).astype(bf16)
        part_send(0, i, main_at).start()
    own_part[main_at, :] = product(main_at, c, 0, CHUNKS)

    for k in range(CHUNKS):
        for d in range(max(DIRECT + 1, chips - far), chips):
            arrive(d, k)
        for i in range(far):
            from_partner(tail_first + i, k)
        for i in range(n_col):
            j = peer(i)
            part = product(tail_at, j, k, 1)
            if k > 0:
                part = part + tail_acc[i]
            if k < CHUNKS - 1:
                tail_acc[i] = part
            elif i < n_col - 1:
                part_out[i, tail_at, :] = part.astype(bf16)
                part_send(1, i, tail_at).start()
            else:
                own_part[tail_at, :] = part

    for j in range(student_gain.shape[0]):
        sgain[:, j * LANES:(j + 1) * LANES] = student_gain[j:j + 1, :]
    gain_rows = width // LANES
    for j in range(gain_rows):
        tgain[:, j * LANES:(j + 1) * LANES] = teacher_gain[pl.ds(me * gain_rows + j, 1), :]

    res_copy.wait()
    for i in range(n_col - 1):
        j = peer(i)
        done(res_place(j), col_recv.at[0, j])

    def gather_parts(stage, at, rows):
        for i in range(n_col - 1):
            j = peer(i)
            done(part_in.at[j, at, :], col_recv.at[1 + stage, j])
        summed = own_part[at, :] + res[at, :].astype(f32)
        for i in range(n_col - 1):
            summed = summed + part_in[peer(i), at, :].astype(f32)
        total[at, :] = summed
        squares[at, :] = jnp.broadcast_to(jnp.sum(summed * summed, axis=1, keepdims=True), (rows, LANES))

    gather_parts(0, main_at, main_rows)

    for i in range(chips):
        pos = (p + i) % chips
        done(row_slots(pos * 2 + 1 - core), hid_row.at[pos])

    tile = 16
    eight = 8 // hid_rows if hid_rows < 8 else 1
    per = tile // hid_rows

    def normalize(t, _):
        at = pl.ds(pl.multiple_of(t * tile, tile), tile)
        x = jnp.concatenate(
            [
                jnp.concatenate([hid[t * per + g + i].astype(f32) for i in range(eight)], axis=0)
                for g in range(0, per, eight)
            ],
            axis=0,
        )
        x = x * lax.rsqrt(jnp.mean(x * x, axis=1, keepdims=True) + norm_eps)
        normed[at, :] = x
        student[at, :] = (x * sgain[...]).astype(bf16)
        return 0

    lax.fori_loop(0, tokens // tile, normalize, 0)

    gather_parts(1, tail_at, tail_rows)
    for b in range(tokens // LANES):
        lanes = slice(b * LANES, (b + 1) * LANES)
        row = jnp.transpose(squares[lanes, :])[0:1, :]
        sq_out[:, lanes] = row
        sq_in[me, :, lanes] = row

    def send_sq(i, _):
        d = (me + 1 + i) % devices
        remote(sq_out, sq_in.at[me], all_send.at[0], all_recv.at[0], (d // n_col, d % n_col)).start()
        return 0

    lax.fori_loop(0, devices - 1, send_sq, 0)

    proj_copy.wait()
    predicted[...] = jnp.dot(student[...], proj[...], preferred_element_type=f32)
    both[0:tokens, :] = predicted[...].astype(bf16)
    both[tokens:, :] = (total[...] * tgain[...]).astype(bf16)
    step = 512

    def early(n, _):
        at = pl.ds(pl.multiple_of(n * step, step), step)
        back = lax.dot_general(
            both[...], proj[at, :], (((1,), (1,)), ((), ())), preferred_element_type=f32
        )
        x = normed[:, at]
        fixed[:, at] = jnp.sum(back[0:tokens, :] * x, axis=0, keepdims=True)
        normed[:, at] = back[tokens:, :] * x
        return 0

    lax.fori_loop(0, d_s // step, early, 0)

    others = sq_in.at[pl.ds(0, devices - 1)]
    done(others, all_recv.at[0])
    factor = lax.rsqrt(jnp.sum(sq_in[...], axis=0) / d_t + norm_eps)
    blocks = [slice(b * LANES, (b + 1) * LANES) for b in range(tokens // LANES)]
    scales = [jnp.transpose(jnp.broadcast_to(factor[:, lanes], (LANES, LANES))) for lanes in blocks]
    half = d_s // LANES // 2
    for q in range(2 * half):
        lanes = slice(q * LANES, (q + 1) * LANES)
        moved = jnp.zeros((1, LANES), f32)
        for at, scale in zip(blocks, scales):
            moved = moved + jnp.sum(normed[at, lanes] * scale, axis=0, keepdims=True)
        gp[q // half, q % half:q % half + 1, :] = (fixed[:, lanes] - moved) * (1.0 / 64.0)
    loss_part = jnp.zeros((1, 1), f32)
    for at, scale in zip(blocks, scales):
        target = (total[at, :] * scale[:, 0:1] * tgain[...]).astype(bf16)
        difference = predicted[at, :] - target.astype(f32)
        loss_part = loss_part + jnp.sum(difference * difference, keepdims=True)
        error[at, :] = (difference * (1.0 / 64.0)).astype(bf16)
    loss_row = jnp.broadcast_to(loss_part, (1, LANES))
    gp[0, half:half + 1, :] = loss_row
    gp[1, half:half + 1, :] = loss_row

    give = remote(gp.at[1 - core], gp_in, pair_send.at[0], pair_recv.at[0], partner)
    give.start()
    give.wait_recv()
    place = p * n_col + c
    gs[...] = gp[core] + gp_in[...]
    gs_in[place] = gs[...]
    count = chips * n_col

    def send_gain(i, _):
        d = (place + 1 + i) % count
        remote(
            gs, gs_in.at[place], all_send.at[1], all_recv.at[1], ((d // n_col) * 2 + core, d % n_col)
        ).start()
        return 0

    lax.fori_loop(0, count - 1, send_gain, 0)
    rest = gs_in.at[pl.ds(0, count - 1)]

    def project(i, _):
        at = pl.ds(pl.multiple_of(i * step, step), step)
        grad_out[at, :] = lax.dot_general(
            student[:, at], error[...], (((0,), (0,)), ((), ())), preferred_element_type=f32
        )
        return 0

    lax.fori_loop(0, d_s // step, project, 0)
    for k in range(CHUNKS):
        for way in range(2):
            sign = 1 - 2 * way
            for d in range(1, min(DIRECT, chips - 1) + 1):
                @pl.when(inside(p + sign * d))
                def _(way=way, d=d, k=k):
                    done(context.at[:, cols_of(k)], ctx_send.at[way, d - 1, k])
            for d in range(DIRECT, chips):
                pos = p - sign * d

                @pl.when(inside(pos) & inside(p + sign))
                def _(way=way, pos=pos, k=k):
                    done(block(pos, k), ctx_fwd.at[way, pos, k])
        for pos in range(chips):
            done(block(pos, k), ctx_side.at[pos, k])
    for i in range(chips - 1):
        done(hidden, hid_z.at[i])
    for i in range(n_col - 1):
        for pos in range(chips):
            done(slot(pos, c), hid_side.at[i, pos])
        done(res_part(peer(i)), col_send.at[0, i])
        done(part_out.at[i, main_at, :], col_send.at[1, i])
        done(part_out.at[i, tail_at, :], col_send.at[2, i])
    for pos in range(chips):
        done(row_slots(pos * 2 + core), hid_pair.at[pos])
    done(others, all_send.at[0])
    give.wait_send()

    done(rest, all_recv.at[1])
    final[core] = jnp.sum(gs_in[...], axis=0)
    swap = remote(final.at[core], final.at[core], pair_send.at[1], pair_recv.at[1], partner)
    swap.start()
    done(rest, all_send.at[1])
    loss_out[...] = final[core, half:half + 1, :] / (tokens * d_t)
    done(final.at[1 - core], pair_recv.at[1])
    gain_out[0:half, :] = final[0, 0:half, :]
    gain_out[half:, :] = final[1, 0:half, :]
    swap.wait_send()


def store(grad, gain_in, loss_in, grad_out, gain_out, loss_out, sem):
    steps = sem.shape[0] - 2
    size = grad.shape[0] // steps
    copies = []
    for i in range(steps):
        rows = pl.ds(i * size, size)
        copies.append(pltpu.make_async_copy(grad.at[rows, :], grad_out.at[rows, :], sem.at[i]))
    copies.append(pltpu.make_async_copy(gain_in, gain_out, sem.at[steps]))
    copies.append(pltpu.make_async_copy(loss_in, loss_out, sem.at[steps + 1]))
    for copy in copies:
        copy.start()
    for copy in copies:
        copy.wait()


def store_call(grad, gain, loss, room):
    hbm = pl.BlockSpec(memory_space=pltpu.HBM)
    return pl.pallas_call(
        store,
        out_shape=tuple(jax.ShapeDtypeStruct(a.shape, a.dtype) for a in (grad, gain, loss)),
        in_specs=[pl.BlockSpec(memory_space=pltpu.VMEM), hbm, hbm],
        out_specs=(hbm,) * 3,
        scratch_shapes=[pltpu.SemaphoreType.DMA((STORES + 2,))],
        compiler_params=pltpu.CompilerParams(vmem_limit_bytes=room),
    )(pltpu.with_memory_space_constraint(grad, pltpu.VMEM), gain, loss)


def per_device(
    n_row, n_col,
    context, out_weight, residual, teacher_gain, student_hidden, student_gain, projector,
):
    devices = n_row * n_col
    chips = n_row // 2
    tokens = context.shape[0] * n_row
    d_s, width = projector.shape
    half = d_s // LANES // 2
    f32, bf16 = jnp.float32, jnp.bfloat16
    anywhere = pl.BlockSpec(memory_space=pl.ANY)
    vmem = pl.BlockSpec(memory_space=pltpu.VMEM)
    dma = pltpu.SemaphoreType.DMA
    room = 67_000_000 - d_s * width * 4
    grad_proj, grad_gain, loss = pl.pallas_call(
        functools.partial(body, n_row, n_col),
        out_shape=(
            pltpu.VMEM((d_s, width), f32),
            jax.ShapeDtypeStruct((2 * half, LANES), f32),
            jax.ShapeDtypeStruct((1, LANES), f32),
        ),
        in_specs=[anywhere, anywhere, anywhere, vmem, anywhere, vmem, anywhere],
        out_specs=(vmem, vmem, vmem),
        scratch_shapes=[
            pltpu.VMEM((tokens, d_s), bf16),
            pltpu.VMEM((tokens, width), bf16),
            pltpu.VMEM((tokens, context.shape[1]), bf16),
            pltpu.VMEM(out_weight.shape, bf16),
            pltpu.VMEM((d_s, width), bf16),
            pltpu.VMEM((n_col, max(1, chips // 4) * 2 * context.shape[0], width), f32),
            pltpu.VMEM((tokens, width), f32),
            pltpu.VMEM((n_col - 1, tokens, width), bf16),
            pltpu.VMEM((n_col, tokens, width), bf16),
            pltpu.VMEM((tokens, width), bf16),
            pltpu.VMEM((devices,) + student_hidden.shape, bf16),
            pltpu.VMEM((tokens, d_s), f32),
            pltpu.VMEM((1, d_s), f32),
            pltpu.VMEM((1, width), f32),
            pltpu.VMEM((tokens, width), f32),
            pltpu.VMEM((tokens, width), f32),
            pltpu.VMEM((2 * tokens, width), bf16),
            pltpu.VMEM((tokens, LANES), f32),
            pltpu.VMEM((1, tokens), f32),
            pltpu.VMEM((devices, 1, tokens), f32),
            pltpu.VMEM((1, d_s), f32),
            pltpu.VMEM((2, half + 1, LANES), f32),
            pltpu.VMEM((half + 1, LANES), f32),
            pltpu.VMEM((half + 1, LANES), f32),
            pltpu.VMEM((chips * n_col, half + 1, LANES), f32),
            pltpu.VMEM((2, half + 1, LANES), f32),
            dma((6,)),
            dma((CHUNKS,)),
            dma((2, DIRECT, CHUNKS)),
            dma((2, chips, CHUNKS)),
            dma((chips, CHUNKS)),
            dma((n_row, CHUNKS)),
            dma((chips,)),
            dma((n_col, chips)),
            dma((chips,)),
            dma((chips, n_col)),
            dma((chips,)),
            dma((3, n_col)),
            dma((3, n_col)),
            dma((2,)),
            dma((2,)),
            dma((2,)),
            dma((2,)),
        ],
        compiler_params=pltpu.CompilerParams(
            collective_id=0, has_side_effects=True, vmem_limit_bytes=room
        ),
    )(
        context, out_weight, residual, teacher_gain.reshape(-1, LANES), student_hidden,
        student_gain.reshape(-1, LANES), projector,
    )
    grad_proj, grad_gain, loss = store_call(grad_proj, grad_gain, loss, room)
    return (grad_proj, grad_gain.reshape(-1), loss[0, 0])


def solution(mesh):
    placed = (
        P("row", "col"),
        P("col", "row"),
        P("col", "row"),
        P(),
        P(("row", "col"), None),
        P(),
        P(None, ("row", "col")),
    )
    return jax.shard_map(
        functools.partial(per_device, mesh.shape["row"], mesh.shape["col"]),
        mesh=mesh,
        in_specs=placed,
        out_specs=(P(None, ("row", "col")), P(), P()),
        check_vma=False,
    )
```

```python
import functools

import jax
import jax.numpy as jnp
from jax import lax
from jax.experimental import pallas as pl
from jax.experimental.pallas import tpu as pltpu
from jax.sharding import PartitionSpec as P

norm_eps = 1e-05
LANES = 128
CHUNKS = 1
DIRECT = 2
STORES = 8
MESH = pl.DeviceIdType.MESH


def body(
    n_row, n_col,
    context, weight, residual, teacher_gain, hidden, student_gain, projector,
    grad_out, gain_out, loss_out,
    student, error, ctx, w, proj, own_part, part_out, part_in, res, hid, normed, sgain, tgain,
    predicted, total, both, squares, sq_out, sq_in, fixed, gp, gp_in, gs, gs_in, final,
    local_sem, w_sem, ctx_send, ctx_fwd, ctx_side, ctx_recv, hid_z, hid_side, hid_pair, hid_recv, hid_row,
    col_send, col_recv, all_send, all_recv, pair_send, pair_recv,
):
    devices = n_row * n_col
    chips = n_row // 2
    r, c = lax.axis_index("row"), lax.axis_index("col")
    me = r * n_col + c
    p, core = r // 2, r % 2
    tok, features = context.shape
    chunk = features // CHUNKS
    tokens = tok * n_row
    width = proj.shape[1]
    res_rows = residual.shape[0]
    hid_rows, d_s = hidden.shape
    d_t = width * devices
    f32, bf16 = jnp.float32, jnp.bfloat16
    partner = (r + 1 - 2 * core, c)

    main_at, main_rows = pl.ds(0, tokens), tokens

    def turn(size):
        return jnp.where(p < chips // 2, size - 1, 1)

    def peer(i):
        return (c + 1 + i) % n_col

    def same_core(i):
        return ((p + 1 + i) % chips) * 2 + core

    def remote(src, dst, send_sem, recv_sem, device):
        return pltpu.make_async_remote_copy(
            src_ref=src, dst_ref=dst, send_sem=send_sem, recv_sem=recv_sem,
            device_id=device, device_id_type=MESH,
        )

    def done(ref, sem):
        pltpu.make_async_copy(ref, ref, sem).wait()

    barrier = pltpu.get_barrier_semaphore()

    def greet(device):
        pl.semaphore_signal(barrier, inc=1, device_id=device, device_id_type=MESH)

    greet(partner)
    for i in range(chips - 1):
        greet((same_core(i), c))
    for i in range(n_col - 1):
        greet((r, peer(i)))

    def rows_of(row):
        return pl.ds(pl.multiple_of(row * tok, tok), tok)

    def cols_of(k):
        return pl.ds(k * chunk, chunk)

    def res_place(j):
        return res.at[pl.ds(pl.multiple_of(j * res_rows, res_rows), res_rows), :]

    def res_part(j):
        return residual.at[:, pl.ds(pl.multiple_of(j * width, width), width)]

    ctx_copy = pltpu.make_async_copy(context, ctx.at[rows_of(r), :], local_sem.at[0])
    hid_copy = pltpu.make_async_copy(hidden, hid.at[me], local_sem.at[1])
    res_copy = pltpu.make_async_copy(res_part(c), res_place(c), local_sem.at[2])
    proj_copy = pltpu.make_async_copy(projector, proj, local_sem.at[3])
    ctx_copy.start()
    hid_copy.start()

    def w_copy(k):
        part = pl.ds(k * chunk, chunk)
        return pltpu.make_async_copy(weight.at[part, :], w.at[part, :], w_sem.at[k])

    for k in range(CHUNKS):
        w_copy(k).start()
    res_copy.start()
    proj_copy.start()
    pl.semaphore_wait(barrier, 1 + chips - 1 + n_col - 1)

    def inside(pos):
        return (pos >= 0) & (pos < chips)

    def block(pos, k):
        return ctx.at[rows_of(pos * 2 + core), cols_of(k)]

    def ctx_direct(way, d, k):
        sign = 1 - 2 * way
        return remote(
            context.at[:, cols_of(k)], block(p, k), ctx_send.at[way, d - 1, k], ctx_recv.at[r, k],
            ((p + sign * d) * 2 + core, c),
        )

    def ctx_onward(way, pos, k):
        sign = 1 - 2 * way
        return remote(
            block(pos, k), block(pos, k), ctx_fwd.at[way, pos, k], ctx_recv.at[pos * 2 + core, k],
            ((p + sign) * 2 + core, c),
        )

    def ctx_across(pos, k, first=False):
        src = context.at[:, cols_of(k)] if first else block(pos, k)
        return remote(src, block(pos, k), ctx_side.at[pos, k], ctx_recv.at[pos * 2 + core, k], partner)

    def slot(pos, col):
        return hid.at[(pos * 2 + core) * n_col + col]

    def row_slots(row):
        return hid.at[pl.ds(pl.multiple_of(row * n_col, n_col), n_col)]

    def hid_to_z(i):
        return remote(hidden, slot(p, c), hid_z.at[i], hid_recv.at[p, c], (same_core(i), c))

    def hid_to_side(pos, i, first=False):
        src = hidden if first else slot(pos, c)
        return remote(src, slot(pos, c), hid_side.at[i, pos], hid_recv.at[pos, c], (r, peer(i)))

    def hid_to_pair(pos):
        row = pos * 2 + core
        return remote(row_slots(row), row_slots(row), hid_pair.at[pos], hid_row.at[pos], partner)

    def res_send(i):
        return remote(res_part(peer(i)), res_place(c), col_send.at[0, i], col_recv.at[0, c], (r, peer(i)))

    for i in range(chips - 1):
        hid_to_z(i).start()
    for i in range(n_col - 1):
        hid_to_side(p, i, True).start()
    for d in range(min(DIRECT, chips - 1), 0, -1):
        for k in range(CHUNKS):
            for way in range(2):
                @pl.when(inside(p + (1 - 2 * way) * d))
                def _(way=way, d=d, k=k):
                    ctx_direct(way, d, k).start()
    for k in range(CHUNKS):
        ctx_across(p, k, True).start()

    def arrive(d, k):
        for way in range(2):
            sign = 1 - 2 * way
            pos = p - sign * d

            @pl.when(inside(pos))
            def _(way=way, sign=sign, pos=pos):
                done(block(pos, k), ctx_recv.at[pos * 2 + core, k])
                if d >= DIRECT:
                    @pl.when(inside(p + sign))
                    def _():
                        ctx_onward(way, pos, k).start()
                ctx_across(pos, k).start()

    for i in range(chips - 1):
        pos = (p + 1 + i) % chips
        done(slot(pos, c), hid_recv.at[pos, c])
        for q in range(n_col - 1):
            hid_to_side(pos, q).start()

    for i in range(n_col - 1):
        res_send(i).start()
    for k in range(CHUNKS):
        arrive(DIRECT, k)
    for d in range(1, DIRECT):
        for k in range(CHUNKS):
            arrive(d, k)

    def from_partner(pos, k):
        row = pos * 2 + 1 - core
        done(ctx.at[rows_of(row), cols_of(k)], ctx_recv.at[row, k])

    def part_send(stage, i, at):
        return remote(
            part_out.at[i, at, :], part_in.at[c, at, :], col_send.at[1 + stage, i],
            col_recv.at[1 + stage, c], (r, peer(i)),
        )

    def product(at, j, first, count):
        rows = slice(first * chunk, (first + count) * chunk)
        cols = pl.ds(pl.multiple_of(j * width, width), width)
        return jnp.dot(ctx[at, rows], w[rows, cols], preferred_element_type=f32)

    hid_copy.wait()
    for i in range(chips):
        pos = (p + i) % chips
        for q in range(n_col - 1):
            j = peer(q)
            done(slot(pos, j), hid_recv.at[pos, j])
        hid_to_pair(pos).start()

    for j in range(student_gain.shape[0]):
        sgain[:, j * LANES:(j + 1) * LANES] = student_gain[j:j + 1, :]
    gain_rows = width // LANES
    for j in range(gain_rows):
        tgain[:, j * LANES:(j + 1) * LANES] = teacher_gain[pl.ds(me * gain_rows + j, 1), :]

    for d in range(DIRECT + 1, chips):
        for k in range(CHUNKS):
            arrive(d, k)
    ctx_copy.wait()
    for k in range(CHUNKS):
        for i in range(chips):
            from_partner(i, k)
        w_copy(k).wait()
    for i in range(n_col - 1):
        part_out[i, main_at, :] = product(main_at, peer(i), 0, CHUNKS).astype(bf16)
        part_send(0, i, main_at).start()
    own_part[main_at, :] = product(main_at, c, 0, CHUNKS)

    res_copy.wait()
    for i in range(n_col - 1):
        j = peer(i)
        done(res_place(j), col_recv.at[0, j])

    def gather_parts(stage, at, rows):
        for i in range(n_col - 1):
            j = peer(i)
            done(part_in.at[j, at, :], col_recv.at[1 + stage, j])
        summed = own_part[at, :] + res[at, :].astype(f32)
        for i in range(n_col - 1):
            summed = summed + part_in[peer(i), at, :].astype(f32)
        total[at, :] = summed
        squares[at, :] = jnp.broadcast_to(jnp.sum(summed * summed, axis=1, keepdims=True), (rows, LANES))

    for i in range(chips):
        pos = (p + i) % chips
        done(row_slots(pos * 2 + 1 - core), hid_row.at[pos])

    tile = 16
    eight = 8 // hid_rows if hid_rows < 8 else 1
    per = tile // hid_rows

    def normalize(t, _):
        at = pl.ds(pl.multiple_of(t * tile, tile), tile)
        x = jnp.concatenate(
            [
                jnp.concatenate([hid[t * per + g + i].astype(f32) for i in range(eight)], axis=0)
                for g in range(0, per, eight)
            ],
            axis=0,
        )
        x = x * lax.rsqrt(jnp.mean(x * x, axis=1, keepdims=True) + norm_eps)
        normed[at, :] = x
        student[at, :] = (x * sgain[...]).astype(bf16)
        return 0

    lax.fori_loop(0, tokens // tile, normalize, 0)

    proj_copy.wait()
    predicted[...] = jnp.dot(student[...], proj[...], preferred_element_type=f32)
    gather_parts(0, main_at, main_rows)

    for b in range(tokens // LANES):
        lanes = slice(b * LANES, (b + 1) * LANES)
        row = jnp.transpose(squares[lanes, :])[0:1, :]
        sq_out[:, lanes] = row
        sq_in[me, :, lanes] = row

    def send_sq(i, _):
        d = (me + turn(devices) * (1 + i)) % devices
        remote(sq_out, sq_in.at[me], all_send.at[0], all_recv.at[0], (d // n_col, d % n_col)).start()
        return 0

    lax.fori_loop(0, devices - 1, send_sq, 0)

    both[0:tokens, :] = predicted[...].astype(bf16)
    both[tokens:, :] = (total[...] * tgain[...]).astype(bf16)
    step = 512

    def early(n, _):
        at = pl.ds(pl.multiple_of(n * step, step), step)
        back = lax.dot_general(
            both[...], proj[at, :], (((1,), (1,)), ((), ())), preferred_element_type=f32
        )
        x = normed[:, at]
        fixed[:, at] = jnp.sum(back[0:tokens, :] * x, axis=0, keepdims=True)
        normed[:, at] = back[tokens:, :] * x
        return 0

    lax.fori_loop(0, d_s // step, early, 0)

    others = sq_in.at[pl.ds(0, devices - 1)]
    done(others, all_recv.at[0])
    factor = lax.rsqrt(jnp.sum(sq_in[...], axis=0) / d_t + norm_eps)
    blocks = [slice(b * LANES, (b + 1) * LANES) for b in range(tokens // LANES)]
    scales = [jnp.transpose(jnp.broadcast_to(factor[:, lanes], (LANES, LANES))) for lanes in blocks]
    half = d_s // LANES // 2
    for q in range(2 * half):
        lanes = slice(q * LANES, (q + 1) * LANES)
        moved = jnp.zeros((1, LANES), f32)
        for at, scale in zip(blocks, scales):
            moved = moved + jnp.sum(normed[at, lanes] * scale, axis=0, keepdims=True)
        gp[q // half, q % half:q % half + 1, :] = (fixed[:, lanes] - moved) * (1.0 / 64.0)
    loss_part = jnp.zeros((1, 1), f32)
    for at, scale in zip(blocks, scales):
        target = (total[at, :] * scale[:, 0:1] * tgain[...]).astype(bf16)
        difference = predicted[at, :] - target.astype(f32)
        loss_part = loss_part + jnp.sum(difference * difference, keepdims=True)
        error[at, :] = (difference * (1.0 / 64.0)).astype(bf16)
    loss_row = jnp.broadcast_to(loss_part, (1, LANES))
    gp[0, half:half + 1, :] = loss_row
    gp[1, half:half + 1, :] = loss_row

    give = remote(gp.at[1 - core], gp_in, pair_send.at[0], pair_recv.at[0], partner)
    give.start()
    give.wait_recv()
    place = p * n_col + c
    gs[...] = gp[core] + gp_in[...]
    gs_in[place] = gs[...]
    count = chips * n_col

    def send_gain(i, _):
        d = (place + turn(count) * (1 + i)) % count
        remote(
            gs, gs_in.at[place], all_send.at[1], all_recv.at[1], ((d // n_col) * 2 + core, d % n_col)
        ).start()
        return 0

    lax.fori_loop(0, count - 1, send_gain, 0)
    rest = gs_in.at[pl.ds(0, count - 1)]

    def project(i, _):
        at = pl.ds(pl.multiple_of(i * step, step), step)
        grad_out[at, :] = lax.dot_general(
            student[:, at], error[...], (((0,), (0,)), ((), ())), preferred_element_type=f32
        )
        return 0

    lax.fori_loop(0, d_s // step, project, 0)
    for k in range(CHUNKS):
        for way in range(2):
            sign = 1 - 2 * way
            for d in range(1, min(DIRECT, chips - 1) + 1):
                @pl.when(inside(p + sign * d))
                def _(way=way, d=d, k=k):
                    done(context.at[:, cols_of(k)], ctx_send.at[way, d - 1, k])
            for d in range(DIRECT, chips):
                pos = p - sign * d

                @pl.when(inside(pos) & inside(p + sign))
                def _(way=way, pos=pos, k=k):
                    done(block(pos, k), ctx_fwd.at[way, pos, k])
        for pos in range(chips):
            done(block(pos, k), ctx_side.at[pos, k])
    for i in range(chips - 1):
        done(hidden, hid_z.at[i])
    for i in range(n_col - 1):
        for pos in range(chips):
            done(slot(pos, c), hid_side.at[i, pos])
        done(res_part(peer(i)), col_send.at[0, i])
        done(part_out.at[i, main_at, :], col_send.at[1, i])
    for pos in range(chips):
        done(row_slots(pos * 2 + core), hid_pair.at[pos])
    done(others, all_send.at[0])
    give.wait_send()

    done(rest, all_recv.at[1])
    final[core] = jnp.sum(gs_in[...], axis=0)
    swap = remote(final.at[core], final.at[core], pair_send.at[1], pair_recv.at[1], partner)
    swap.start()
    done(rest, all_send.at[1])
    loss_out[...] = final[core, half:half + 1, :] / (tokens * d_t)
    done(final.at[1 - core], pair_recv.at[1])
    gain_out[0:half, :] = final[0, 0:half, :]
    gain_out[half:, :] = final[1, 0:half, :]
    swap.wait_send()


def store(grad, gain_in, loss_in, grad_out, gain_out, loss_out, sem):
    steps = sem.shape[0] - 2
    size = grad.shape[0] // steps
    copies = []
    for i in range(steps):
        rows = pl.ds(i * size, size)
        copies.append(pltpu.make_async_copy(grad.at[rows, :], grad_out.at[rows, :], sem.at[i]))
    copies.append(pltpu.make_async_copy(gain_in, gain_out, sem.at[steps]))
    copies.append(pltpu.make_async_copy(loss_in, loss_out, sem.at[steps + 1]))
    for copy in copies:
        copy.start()
    for copy in copies:
        copy.wait()


def store_call(grad, gain, loss, room):
    hbm = pl.BlockSpec(memory_space=pltpu.HBM)
    return pl.pallas_call(
        store,
        out_shape=tuple(jax.ShapeDtypeStruct(a.shape, a.dtype) for a in (grad, gain, loss)),
        in_specs=[pl.BlockSpec(memory_space=pltpu.VMEM), hbm, hbm],
        out_specs=(hbm,) * 3,
        scratch_shapes=[pltpu.SemaphoreType.DMA((STORES + 2,))],
        compiler_params=pltpu.CompilerParams(vmem_limit_bytes=room),
    )(pltpu.with_memory_space_constraint(grad, pltpu.VMEM), gain, loss)


def per_device(
    n_row, n_col,
    context, out_weight, residual, teacher_gain, student_hidden, student_gain, projector,
):
    devices = n_row * n_col
    chips = n_row // 2
    tokens = context.shape[0] * n_row
    d_s, width = projector.shape
    half = d_s // LANES // 2
    f32, bf16 = jnp.float32, jnp.bfloat16
    anywhere = pl.BlockSpec(memory_space=pl.ANY)
    vmem = pl.BlockSpec(memory_space=pltpu.VMEM)
    dma = pltpu.SemaphoreType.DMA
    room = 67_000_000 - d_s * width * 4
    grad_proj, grad_gain, loss = pl.pallas_call(
        functools.partial(body, n_row, n_col),
        out_shape=(
            pltpu.VMEM((d_s, width), f32),
            jax.ShapeDtypeStruct((2 * half, LANES), f32),
            jax.ShapeDtypeStruct((1, LANES), f32),
        ),
        in_specs=[anywhere, anywhere, anywhere, vmem, anywhere, vmem, anywhere],
        out_specs=(vmem, vmem, vmem),
        scratch_shapes=[
            pltpu.VMEM((tokens, d_s), bf16),
            pltpu.VMEM((tokens, width), bf16),
            pltpu.VMEM((tokens, context.shape[1]), bf16),
            pltpu.VMEM(out_weight.shape, bf16),
            pltpu.VMEM((d_s, width), bf16),
            pltpu.VMEM((tokens, width), f32),
            pltpu.VMEM((n_col - 1, tokens, width), bf16),
            pltpu.VMEM((n_col, tokens, width), bf16),
            pltpu.VMEM((tokens, width), bf16),
            pltpu.VMEM((devices,) + student_hidden.shape, bf16),
            pltpu.VMEM((tokens, d_s), f32),
            pltpu.VMEM((1, d_s), f32),
            pltpu.VMEM((1, width), f32),
            pltpu.VMEM((tokens, width), f32),
            pltpu.VMEM((tokens, width), f32),
            pltpu.VMEM((2 * tokens, width), bf16),
            pltpu.VMEM((tokens, LANES), f32),
            pltpu.VMEM((1, tokens), f32),
            pltpu.VMEM((devices, 1, tokens), f32),
            pltpu.VMEM((1, d_s), f32),
            pltpu.VMEM((2, half + 1, LANES), f32),
            pltpu.VMEM((half + 1, LANES), f32),
            pltpu.VMEM((half + 1, LANES), f32),
            pltpu.VMEM((chips * n_col, half + 1, LANES), f32),
            pltpu.VMEM((2, half + 1, LANES), f32),
            dma((6,)),
            dma((CHUNKS,)),
            dma((2, DIRECT, CHUNKS)),
            dma((2, chips, CHUNKS)),
            dma((chips, CHUNKS)),
            dma((n_row, CHUNKS)),
            dma((chips,)),
            dma((n_col, chips)),
            dma((chips,)),
            dma((chips, n_col)),
            dma((chips,)),
            dma((3, n_col)),
            dma((3, n_col)),
            dma((2,)),
            dma((2,)),
            dma((2,)),
            dma((2,)),
        ],
        compiler_params=pltpu.CompilerParams(
            collective_id=0, has_side_effects=True, vmem_limit_bytes=room
        ),
    )(
        context, out_weight, residual, teacher_gain.reshape(-1, LANES), student_hidden,
        student_gain.reshape(-1, LANES), projector,
    )
    grad_proj, grad_gain, loss = store_call(grad_proj, grad_gain, loss, room)
    return (grad_proj, grad_gain.reshape(-1), loss[0, 0])


def solution(mesh):
    placed = (
        P("row", "col"),
        P("col", "row"),
        P("col", "row"),
        P(),
        P(("row", "col"), None),
        P(),
        P(None, ("row", "col")),
    )
    return jax.shard_map(
        functools.partial(per_device, mesh.shape["row"], mesh.shape["col"]),
        mesh=mesh,
        in_specs=placed,
        out_specs=(P(None, ("row", "col")), P(), P()),
        check_vma=False,
    )
```

```python
import functools

import jax
import jax.numpy as jnp
from jax import lax
from jax.experimental import pallas as pl
from jax.experimental.pallas import tpu as pltpu
from jax.sharding import PartitionSpec as P

norm_eps = 1e-05
LANES = 128
CHUNKS = 1
DIRECT = 2
STORES = 8
MESH = pl.DeviceIdType.MESH


def body(
    n_row, n_col,
    context, weight, residual, teacher_gain, hidden, student_gain, projector,
    grad_out, gain_out, loss_out,
    student, error, ctx, w, proj, own_part, part_out, part_in, res, hid, normed, sgain, tgain,
    predicted, total, both, squares, sq_out, sq_in, fixed, gp, gp_in, gs, gs_in, final,
    local_sem, w_sem, ctx_send, ctx_fwd, ctx_side, ctx_recv, hid_z, hid_side, hid_pair, hid_recv, hid_row,
    col_send, col_recv, all_send, all_recv, pair_send, pair_recv,
):
    devices = n_row * n_col
    chips = n_row // 2
    r, c = lax.axis_index("row"), lax.axis_index("col")
    me = r * n_col + c
    p, core = r // 2, r % 2
    tok, features = context.shape
    chunk = features // CHUNKS
    tokens = tok * n_row
    width = proj.shape[1]
    res_rows = residual.shape[0]
    hid_rows, d_s = hidden.shape
    d_t = width * devices
    f32, bf16 = jnp.float32, jnp.bfloat16
    partner = (r + 1 - 2 * core, c)

    main_at, main_rows = pl.ds(0, tokens), tokens

    def turn(size):
        return jnp.where(p < chips // 2, size - 1, 1)

    def peer(i):
        return (c + 1 + i) % n_col

    def same_core(i):
        return ((p + 1 + i) % chips) * 2 + core

    def remote(src, dst, send_sem, recv_sem, device):
        return pltpu.make_async_remote_copy(
            src_ref=src, dst_ref=dst, send_sem=send_sem, recv_sem=recv_sem,
            device_id=device, device_id_type=MESH,
        )

    def done(ref, sem):
        pltpu.make_async_copy(ref, ref, sem).wait()

    barrier = pltpu.get_barrier_semaphore()

    def greet(device):
        pl.semaphore_signal(barrier, inc=1, device_id=device, device_id_type=MESH)

    greet(partner)
    for i in range(chips - 1):
        greet((same_core(i), c))
    for i in range(n_col - 1):
        greet((r, peer(i)))

    def rows_of(row):
        return pl.ds(pl.multiple_of(row * tok, tok), tok)

    def cols_of(k):
        return pl.ds(k * chunk, chunk)

    def res_place(j):
        return res.at[pl.ds(pl.multiple_of(j * res_rows, res_rows), res_rows), :]

    def res_part(j):
        return residual.at[:, pl.ds(pl.multiple_of(j * width, width), width)]

    ctx_copy = pltpu.make_async_copy(context, ctx.at[rows_of(r), :], local_sem.at[0])
    hid_copy = pltpu.make_async_copy(hidden, hid.at[me], local_sem.at[1])
    res_copy = pltpu.make_async_copy(res_part(c), res_place(c), local_sem.at[2])
    proj_copy = pltpu.make_async_copy(projector, proj, local_sem.at[3])
    ctx_copy.start()
    hid_copy.start()

    def w_copy(k):
        part = pl.ds(k * chunk, chunk)
        return pltpu.make_async_copy(weight.at[part, :], w.at[part, :], w_sem.at[k])

    for k in range(CHUNKS):
        w_copy(k).start()
    res_copy.start()
    proj_copy.start()
    pl.semaphore_wait(barrier, 1 + chips - 1 + n_col - 1)

    def inside(pos):
        return (pos >= 0) & (pos < chips)

    def block(pos, k):
        return ctx.at[rows_of(pos * 2 + core), cols_of(k)]

    def ctx_direct(way, d, k):
        sign = 1 - 2 * way
        return remote(
            context.at[:, cols_of(k)], block(p, k), ctx_send.at[way, d - 1, k], ctx_recv.at[r, k],
            ((p + sign * d) * 2 + core, c),
        )

    def ctx_onward(way, pos, k):
        sign = 1 - 2 * way
        return remote(
            block(pos, k), block(pos, k), ctx_fwd.at[way, pos, k], ctx_recv.at[pos * 2 + core, k],
            ((p + sign) * 2 + core, c),
        )

    def ctx_across(pos, k, first=False):
        src = context.at[:, cols_of(k)] if first else block(pos, k)
        return remote(src, block(pos, k), ctx_side.at[pos, k], ctx_recv.at[pos * 2 + core, k], partner)

    def slot(pos, col):
        return hid.at[(pos * 2 + core) * n_col + col]

    def row_slots(row):
        return hid.at[pl.ds(pl.multiple_of(row * n_col, n_col), n_col)]

    def hid_to_z(i):
        return remote(hidden, slot(p, c), hid_z.at[i], hid_recv.at[p, c], (same_core(i), c))

    def hid_to_side(pos, i, first=False):
        src = hidden if first else slot(pos, c)
        return remote(src, slot(pos, c), hid_side.at[i, pos], hid_recv.at[pos, c], (r, peer(i)))

    def hid_to_pair(pos):
        row = pos * 2 + core
        return remote(row_slots(row), row_slots(row), hid_pair.at[pos], hid_row.at[pos], partner)

    def res_send(i):
        return remote(res_part(peer(i)), res_place(c), col_send.at[0, i], col_recv.at[0, c], (r, peer(i)))

    for i in range(chips - 1):
        hid_to_z(i).start()
    for i in range(n_col - 1):
        hid_to_side(p, i, True).start()
    for d in range(min(DIRECT, chips - 1), 0, -1):
        for k in range(CHUNKS):
            for way in range(2):
                @pl.when(inside(p + (1 - 2 * way) * d))
                def _(way=way, d=d, k=k):
                    ctx_direct(way, d, k).start()
    for k in range(CHUNKS):
        ctx_across(p, k, True).start()

    def arrive(d, k):
        for way in range(2):
            sign = 1 - 2 * way
            pos = p - sign * d

            @pl.when(inside(pos))
            def _(way=way, sign=sign, pos=pos):
                done(block(pos, k), ctx_recv.at[pos * 2 + core, k])
                if d >= DIRECT:
                    @pl.when(inside(p + sign))
                    def _():
                        ctx_onward(way, pos, k).start()
                ctx_across(pos, k).start()

    for i in range(chips - 1):
        pos = (p + 1 + i) % chips
        done(slot(pos, c), hid_recv.at[pos, c])
        for q in range(n_col - 1):
            hid_to_side(pos, q).start()

    for i in range(n_col - 1):
        res_send(i).start()
    for k in range(CHUNKS):
        arrive(DIRECT, k)
    for d in range(1, DIRECT):
        for k in range(CHUNKS):
            arrive(d, k)

    def from_partner(pos, k):
        row = pos * 2 + 1 - core
        done(ctx.at[rows_of(row), cols_of(k)], ctx_recv.at[row, k])

    def part_send(stage, i, at):
        return remote(
            part_out.at[i, at, :], part_in.at[c, at, :], col_send.at[1 + stage, i],
            col_recv.at[1 + stage, c], (r, peer(i)),
        )

    def product(at, j, first, count):
        rows = slice(first * chunk, (first + count) * chunk)
        cols = pl.ds(pl.multiple_of(j * width, width), width)
        return jnp.dot(ctx[at, rows], w[rows, cols], preferred_element_type=f32)

    hid_copy.wait()
    for i in range(chips):
        pos = (p + i) % chips
        for q in range(n_col - 1):
            j = peer(q)
            done(slot(pos, j), hid_recv.at[pos, j])
        hid_to_pair(pos).start()

    for j in range(student_gain.shape[0]):
        sgain[:, j * LANES:(j + 1) * LANES] = student_gain[j:j + 1, :]
    gain_rows = width // LANES
    for j in range(gain_rows):
        tgain[:, j * LANES:(j + 1) * LANES] = teacher_gain[pl.ds(me * gain_rows + j, 1), :]

    for d in range(DIRECT + 1, chips):
        for k in range(CHUNKS):
            arrive(d, k)
    ctx_copy.wait()
    for k in range(CHUNKS):
        for i in range(chips):
            from_partner(i, k)
        w_copy(k).wait()
    for i in range(n_col - 1):
        part_out[i, main_at, :] = product(main_at, peer(i), 0, CHUNKS).astype(bf16)
        part_send(0, i, main_at).start()
    own_part[main_at, :] = product(main_at, c, 0, CHUNKS)

    res_copy.wait()
    for i in range(n_col - 1):
        j = peer(i)
        done(res_place(j), col_recv.at[0, j])

    def gather_parts(stage, at, rows):
        for i in range(n_col - 1):
            j = peer(i)
            done(part_in.at[j, at, :], col_recv.at[1 + stage, j])
        summed = own_part[at, :] + res[at, :].astype(f32)
        for i in range(n_col - 1):
            summed = summed + part_in[peer(i), at, :].astype(f32)
        total[at, :] = summed
        squares[at, :] = jnp.broadcast_to(jnp.sum(summed * summed, axis=1, keepdims=True), (rows, LANES))

    for i in range(chips):
        pos = (p + i) % chips
        done(row_slots(pos * 2 + 1 - core), hid_row.at[pos])

    tile = 16
    eight = 8 // hid_rows if hid_rows < 8 else 1
    per = tile // hid_rows

    def normalize(t, _):
        at = pl.ds(pl.multiple_of(t * tile, tile), tile)
        x = jnp.concatenate(
            [
                jnp.concatenate([hid[t * per + g + i].astype(f32) for i in range(eight)], axis=0)
                for g in range(0, per, eight)
            ],
            axis=0,
        )
        x = x * lax.rsqrt(jnp.mean(x * x, axis=1, keepdims=True) + norm_eps)
        normed[at, :] = x
        student[at, :] = (x * sgain[...]).astype(bf16)
        return 0

    lax.fori_loop(0, tokens // tile, normalize, 0)

    proj_copy.wait()
    predicted[...] = jnp.dot(student[...], proj[...], preferred_element_type=f32)
    gather_parts(0, main_at, main_rows)

    for b in range(tokens // LANES):
        lanes = slice(b * LANES, (b + 1) * LANES)
        row = jnp.transpose(squares[lanes, :])[0:1, :]
        sq_out[:, lanes] = row
        sq_in[me, :, lanes] = row

    def send_sq(i, _):
        d = (me + turn(devices) * (1 + i)) % devices
        remote(sq_out, sq_in.at[me], all_send.at[0], all_recv.at[0], (d // n_col, d % n_col)).start()
        return 0

    lax.fori_loop(0, devices - 1, send_sq, 0)

    both[0:tokens, :] = predicted[...].astype(bf16)
    both[tokens:, :] = (total[...] * tgain[...]).astype(bf16)
    step = 512

    def early(n, _):
        at = pl.ds(pl.multiple_of(n * step, step), step)
        back = lax.dot_general(
            both[...], proj[at, :], (((1,), (1,)), ((), ())), preferred_element_type=f32
        )
        x = normed[:, at]
        fixed[:, at] = jnp.sum(back[0:tokens, :] * x, axis=0, keepdims=True)
        normed[:, at] = back[tokens:, :] * x
        return 0

    lax.fori_loop(0, d_s // step, early, 0)

    others = sq_in.at[pl.ds(0, devices - 1)]
    done(others, all_recv.at[0])
    factor = lax.rsqrt(jnp.sum(sq_in[...], axis=0) / d_t + norm_eps)
    blocks = [slice(b * LANES, (b + 1) * LANES) for b in range(tokens // LANES)]
    scales = [jnp.transpose(jnp.broadcast_to(factor[:, lanes], (LANES, LANES))) for lanes in blocks]
    half = d_s // LANES // 2
    for q in range(2 * half):
        lanes = slice(q * LANES, (q + 1) * LANES)
        moved = jnp.zeros((1, LANES), f32)
        for at, scale in zip(blocks, scales):
            moved = moved + jnp.sum(normed[at, lanes] * scale, axis=0, keepdims=True)
        gp[q // half, q % half:q % half + 1, :] = (fixed[:, lanes] - moved) * (1.0 / 64.0)
    gp[:, half:half + 1, :] = jnp.zeros((2, 1, LANES), f32)
    give = remote(gp.at[1 - core], gp_in, pair_send.at[0], pair_recv.at[0], partner)
    give.start()
    loss_part = jnp.zeros((1, 1), f32)
    for at, scale in zip(blocks, scales):
        target = (total[at, :] * scale[:, 0:1] * tgain[...]).astype(bf16)
        difference = predicted[at, :] - target.astype(f32)
        loss_part = loss_part + jnp.sum(difference * difference, keepdims=True)
        error[at, :] = (difference * (1.0 / 64.0)).astype(bf16)

    give.wait_recv()
    place = p * n_col + c
    gs[...] = gp[core] + gp_in[...]
    gs[half:half + 1, :] = jnp.broadcast_to(loss_part, (1, LANES))
    gs_in[place] = gs[...]
    count = chips * n_col

    def send_gain(i, _):
        d = (place + turn(count) * (1 + i)) % count
        remote(
            gs, gs_in.at[place], all_send.at[1], all_recv.at[1], ((d // n_col) * 2 + core, d % n_col)
        ).start()
        return 0

    lax.fori_loop(0, count - 1, send_gain, 0)
    rest = gs_in.at[pl.ds(0, count - 1)]

    def project(i, _):
        at = pl.ds(pl.multiple_of(i * step, step), step)
        grad_out[at, :] = lax.dot_general(
            student[:, at], error[...], (((0,), (0,)), ((), ())), preferred_element_type=f32
        )
        return 0

    lax.fori_loop(0, d_s // step, project, 0)
    for k in range(CHUNKS):
        for way in range(2):
            sign = 1 - 2 * way
            for d in range(1, min(DIRECT, chips - 1) + 1):
                @pl.when(inside(p + sign * d))
                def _(way=way, d=d, k=k):
                    done(context.at[:, cols_of(k)], ctx_send.at[way, d - 1, k])
            for d in range(DIRECT, chips):
                pos = p - sign * d

                @pl.when(inside(pos) & inside(p + sign))
                def _(way=way, pos=pos, k=k):
                    done(block(pos, k), ctx_fwd.at[way, pos, k])
        for pos in range(chips):
            done(block(pos, k), ctx_side.at[pos, k])
    for i in range(chips - 1):
        done(hidden, hid_z.at[i])
    for i in range(n_col - 1):
        for pos in range(chips):
            done(slot(pos, c), hid_side.at[i, pos])
        done(res_part(peer(i)), col_send.at[0, i])
        done(part_out.at[i, main_at, :], col_send.at[1, i])
    for pos in range(chips):
        done(row_slots(pos * 2 + core), hid_pair.at[pos])
    done(others, all_send.at[0])
    give.wait_send()

    done(rest, all_recv.at[1])
    final[core] = jnp.sum(gs_in[...], axis=0)
    swap = remote(final.at[core], final.at[core], pair_send.at[1], pair_recv.at[1], partner)
    swap.start()
    done(rest, all_send.at[1])
    done(final.at[1 - core], pair_recv.at[1])
    loss_out[...] = (final[0, half:half + 1, :] + final[1, half:half + 1, :]) / (tokens * d_t)
    gain_out[0:half, :] = final[0, 0:half, :]
    gain_out[half:, :] = final[1, 0:half, :]
    swap.wait_send()


def store(grad, gain_in, loss_in, grad_out, gain_out, loss_out, sem):
    steps = sem.shape[0] - 2
    size = grad.shape[0] // steps
    copies = []
    for i in range(steps):
        rows = pl.ds(i * size, size)
        copies.append(pltpu.make_async_copy(grad.at[rows, :], grad_out.at[rows, :], sem.at[i]))
    copies.append(pltpu.make_async_copy(gain_in, gain_out, sem.at[steps]))
    copies.append(pltpu.make_async_copy(loss_in, loss_out, sem.at[steps + 1]))
    for copy in copies:
        copy.start()
    for copy in copies:
        copy.wait()


def store_call(grad, gain, loss, room):
    hbm = pl.BlockSpec(memory_space=pltpu.HBM)
    return pl.pallas_call(
        store,
        out_shape=tuple(jax.ShapeDtypeStruct(a.shape, a.dtype) for a in (grad, gain, loss)),
        in_specs=[pl.BlockSpec(memory_space=pltpu.VMEM), hbm, hbm],
        out_specs=(hbm,) * 3,
        scratch_shapes=[pltpu.SemaphoreType.DMA((STORES + 2,))],
        compiler_params=pltpu.CompilerParams(vmem_limit_bytes=room),
    )(pltpu.with_memory_space_constraint(grad, pltpu.VMEM), gain, loss)


def per_device(
    n_row, n_col,
    context, out_weight, residual, teacher_gain, student_hidden, student_gain, projector,
):
    devices = n_row * n_col
    chips = n_row // 2
    tokens = context.shape[0] * n_row
    d_s, width = projector.shape
    half = d_s // LANES // 2
    f32, bf16 = jnp.float32, jnp.bfloat16
    anywhere = pl.BlockSpec(memory_space=pl.ANY)
    vmem = pl.BlockSpec(memory_space=pltpu.VMEM)
    dma = pltpu.SemaphoreType.DMA
    room = 67_000_000 - d_s * width * 4
    grad_proj, grad_gain, loss = pl.pallas_call(
        functools.partial(body, n_row, n_col),
        out_shape=(
            pltpu.VMEM((d_s, width), f32),
            jax.ShapeDtypeStruct((2 * half, LANES), f32),
            jax.ShapeDtypeStruct((1, LANES), f32),
        ),
        in_specs=[anywhere, anywhere, anywhere, vmem, anywhere, vmem, anywhere],
        out_specs=(vmem, vmem, vmem),
        scratch_shapes=[
            pltpu.VMEM((tokens, d_s), bf16),
            pltpu.VMEM((tokens, width), bf16),
            pltpu.VMEM((tokens, context.shape[1]), bf16),
            pltpu.VMEM(out_weight.shape, bf16),
            pltpu.VMEM((d_s, width), bf16),
            pltpu.VMEM((tokens, width), f32),
            pltpu.VMEM((n_col - 1, tokens, width), bf16),
            pltpu.VMEM((n_col, tokens, width), bf16),
            pltpu.VMEM((tokens, width), bf16),
            pltpu.VMEM((devices,) + student_hidden.shape, bf16),
            pltpu.VMEM((tokens, d_s), f32),
            pltpu.VMEM((1, d_s), f32),
            pltpu.VMEM((1, width), f32),
            pltpu.VMEM((tokens, width), f32),
            pltpu.VMEM((tokens, width), f32),
            pltpu.VMEM((2 * tokens, width), bf16),
            pltpu.VMEM((tokens, LANES), f32),
            pltpu.VMEM((1, tokens), f32),
            pltpu.VMEM((devices, 1, tokens), f32),
            pltpu.VMEM((1, d_s), f32),
            pltpu.VMEM((2, half + 1, LANES), f32),
            pltpu.VMEM((half + 1, LANES), f32),
            pltpu.VMEM((half + 1, LANES), f32),
            pltpu.VMEM((chips * n_col, half + 1, LANES), f32),
            pltpu.VMEM((2, half + 1, LANES), f32),
            dma((6,)),
            dma((CHUNKS,)),
            dma((2, DIRECT, CHUNKS)),
            dma((2, chips, CHUNKS)),
            dma((chips, CHUNKS)),
            dma((n_row, CHUNKS)),
            dma((chips,)),
            dma((n_col, chips)),
            dma((chips,)),
            dma((chips, n_col)),
            dma((chips,)),
            dma((3, n_col)),
            dma((3, n_col)),
            dma((2,)),
            dma((2,)),
            dma((2,)),
            dma((2,)),
        ],
        compiler_params=pltpu.CompilerParams(
            collective_id=0, has_side_effects=True, vmem_limit_bytes=room
        ),
    )(
        context, out_weight, residual, teacher_gain.reshape(-1, LANES), student_hidden,
        student_gain.reshape(-1, LANES), projector,
    )
    grad_proj, grad_gain, loss = store_call(grad_proj, grad_gain, loss, room)
    return (grad_proj, grad_gain.reshape(-1), loss[0, 0])


def solution(mesh):
    placed = (
        P("row", "col"),
        P("col", "row"),
        P("col", "row"),
        P(),
        P(("row", "col"), None),
        P(),
        P(None, ("row", "col")),
    )
    return jax.shard_map(
        functools.partial(per_device, mesh.shape["row"], mesh.shape["col"]),
        mesh=mesh,
        in_specs=placed,
        out_specs=(P(None, ("row", "col")), P(), P()),
        check_vma=False,
    )
```

```python
import functools

import jax
import jax.numpy as jnp
from jax import lax
from jax.experimental import pallas as pl
from jax.experimental.pallas import tpu as pltpu
from jax.sharding import PartitionSpec as P

norm_eps = 1e-05
LANES = 128
CHUNKS = 1
DIRECT = 2
STORES = 8
MESH = pl.DeviceIdType.MESH


def body(
    n_row, n_col,
    context, weight, residual, teacher_gain, hidden, student_gain, projector,
    grad_out, gain_out, loss_out,
    student, error, ctx, w, proj, own_part, part_out, part_in, res, hid, normed, sgain, tgain,
    predicted, total, both, squares, sq_out, sq_in, fixed, gp, gp_in, gs, gs_in, final,
    local_sem, w_sem, ctx_send, ctx_fwd, ctx_side, ctx_recv, hid_z, hid_side, hid_pair, hid_recv, hid_row,
    col_send, col_recv, all_send, all_recv, pair_send, pair_recv,
):
    devices = n_row * n_col
    chips = n_row // 2
    r, c = lax.axis_index("row"), lax.axis_index("col")
    me = r * n_col + c
    p, core = r // 2, r % 2
    tok, features = context.shape
    chunk = features // CHUNKS
    tokens = tok * n_row
    width = proj.shape[1]
    res_rows = residual.shape[0]
    hid_rows, d_s = hidden.shape
    d_t = width * devices
    f32, bf16 = jnp.float32, jnp.bfloat16
    partner = (r + 1 - 2 * core, c)

    main_at, main_rows = pl.ds(0, tokens), tokens

    def turn(size):
        return jnp.where(p < chips // 2, size - 1, 1)

    def peer(i):
        return (c + 1 + i) % n_col

    def same_core(i):
        return ((p + 1 + i) % chips) * 2 + core

    def remote(src, dst, send_sem, recv_sem, device):
        return pltpu.make_async_remote_copy(
            src_ref=src, dst_ref=dst, send_sem=send_sem, recv_sem=recv_sem,
            device_id=device, device_id_type=MESH,
        )

    def done(ref, sem):
        pltpu.make_async_copy(ref, ref, sem).wait()

    barrier = pltpu.get_barrier_semaphore()

    def greet(device):
        pl.semaphore_signal(barrier, inc=1, device_id=device, device_id_type=MESH)

    greet(partner)
    for i in range(chips - 1):
        greet((same_core(i), c))
    for i in range(n_col - 1):
        greet((r, peer(i)))

    def rows_of(row):
        return pl.ds(pl.multiple_of(row * tok, tok), tok)

    def cols_of(k):
        return pl.ds(k * chunk, chunk)

    def res_place(j):
        return res.at[pl.ds(pl.multiple_of(j * res_rows, res_rows), res_rows), :]

    def res_part(j):
        return residual.at[:, pl.ds(pl.multiple_of(j * width, width), width)]

    ctx_copy = pltpu.make_async_copy(context, ctx.at[rows_of(r), :], local_sem.at[0])
    hid_copy = pltpu.make_async_copy(hidden, hid.at[me], local_sem.at[1])
    res_copy = pltpu.make_async_copy(res_part(c), res_place(c), local_sem.at[2])
    proj_copy = pltpu.make_async_copy(projector, proj, local_sem.at[3])
    ctx_copy.start()
    hid_copy.start()

    def w_copy(k):
        part = pl.ds(k * chunk, chunk)
        return pltpu.make_async_copy(weight.at[part, :], w.at[part, :], w_sem.at[k])

    for k in range(CHUNKS):
        w_copy(k).start()
    res_copy.start()
    proj_copy.start()
    pl.semaphore_wait(barrier, 1 + chips - 1 + n_col - 1)

    def inside(pos):
        return (pos >= 0) & (pos < chips)

    def block(pos, k):
        return ctx.at[rows_of(pos * 2 + core), cols_of(k)]

    def ctx_direct(way, d, k):
        sign = 1 - 2 * way
        return remote(
            context.at[:, cols_of(k)], block(p, k), ctx_send.at[way, d - 1, k], ctx_recv.at[r, k],
            ((p + sign * d) * 2 + core, c),
        )

    def ctx_onward(way, pos, k):
        sign = 1 - 2 * way
        return remote(
            block(pos, k), block(pos, k), ctx_fwd.at[way, pos, k], ctx_recv.at[pos * 2 + core, k],
            ((p + sign) * 2 + core, c),
        )

    def ctx_across(pos, k, first=False):
        src = context.at[:, cols_of(k)] if first else block(pos, k)
        return remote(src, block(pos, k), ctx_side.at[pos, k], ctx_recv.at[pos * 2 + core, k], partner)

    def slot(pos, col):
        return hid.at[(pos * 2 + core) * n_col + col]

    def row_slots(row):
        return hid.at[pl.ds(pl.multiple_of(row * n_col, n_col), n_col)]

    def hid_to_z(i):
        return remote(hidden, slot(p, c), hid_z.at[i], hid_recv.at[p, c], (same_core(i), c))

    def hid_to_side(pos, i, first=False):
        src = hidden if first else slot(pos, c)
        return remote(src, slot(pos, c), hid_side.at[i, pos], hid_recv.at[pos, c], (r, peer(i)))

    def hid_to_pair(pos):
        row = pos * 2 + core
        return remote(row_slots(row), row_slots(row), hid_pair.at[pos], hid_row.at[pos], partner)

    def res_send(i):
        return remote(res_part(peer(i)), res_place(c), col_send.at[0, i], col_recv.at[0, c], (r, peer(i)))

    for i in range(chips - 1):
        hid_to_z(i).start()
    for i in range(n_col - 1):
        hid_to_side(p, i, True).start()
    for d in range(min(DIRECT, chips - 1), 0, -1):
        for k in range(CHUNKS):
            for way in range(2):
                @pl.when(inside(p + (1 - 2 * way) * d))
                def _(way=way, d=d, k=k):
                    ctx_direct(way, d, k).start()
    for k in range(CHUNKS):
        ctx_across(p, k, True).start()

    def arrive(d, k):
        for way in range(2):
            sign = 1 - 2 * way
            pos = p - sign * d

            @pl.when(inside(pos))
            def _(way=way, sign=sign, pos=pos):
                done(block(pos, k), ctx_recv.at[pos * 2 + core, k])
                if d >= DIRECT:
                    @pl.when(inside(p + sign))
                    def _():
                        ctx_onward(way, pos, k).start()
                ctx_across(pos, k).start()

    for i in range(chips - 1):
        pos = (p + 1 + i) % chips
        done(slot(pos, c), hid_recv.at[pos, c])
        for q in range(n_col - 1):
            hid_to_side(pos, q).start()

    for i in range(n_col - 1):
        res_send(i).start()
    for k in range(CHUNKS):
        arrive(DIRECT, k)
    for d in range(1, DIRECT):
        for k in range(CHUNKS):
            arrive(d, k)

    def from_partner(pos, k):
        row = pos * 2 + 1 - core
        done(ctx.at[rows_of(row), cols_of(k)], ctx_recv.at[row, k])

    def part_send(stage, i, at):
        return remote(
            part_out.at[i, at, :], part_in.at[c, at, :], col_send.at[1 + stage, i],
            col_recv.at[1 + stage, c], (r, peer(i)),
        )

    def product(at, j, first, count):
        rows = slice(first * chunk, (first + count) * chunk)
        cols = pl.ds(pl.multiple_of(j * width, width), width)
        return jnp.dot(ctx[at, rows], w[rows, cols], preferred_element_type=f32)

    hid_copy.wait()
    for i in range(chips):
        pos = (p + i) % chips
        for q in range(n_col - 1):
            j = peer(q)
            done(slot(pos, j), hid_recv.at[pos, j])
        hid_to_pair(pos).start()

    for j in range(student_gain.shape[0]):
        sgain[:, j * LANES:(j + 1) * LANES] = student_gain[j:j + 1, :]
    gain_rows = width // LANES
    for j in range(gain_rows):
        tgain[:, j * LANES:(j + 1) * LANES] = teacher_gain[pl.ds(me * gain_rows + j, 1), :]

    for d in range(DIRECT + 1, chips):
        for k in range(CHUNKS):
            arrive(d, k)
    ctx_copy.wait()
    for k in range(CHUNKS):
        for i in range(chips):
            from_partner(i, k)
        w_copy(k).wait()
    for i in range(n_col - 1):
        part_out[i, main_at, :] = product(main_at, peer(i), 0, CHUNKS).astype(bf16)
        part_send(0, i, main_at).start()
    own_part[main_at, :] = product(main_at, c, 0, CHUNKS)

    res_copy.wait()
    for i in range(n_col - 1):
        j = peer(i)
        done(res_place(j), col_recv.at[0, j])

    def gather_parts(stage, at, rows):
        for i in range(n_col - 1):
            j = peer(i)
            done(part_in.at[j, at, :], col_recv.at[1 + stage, j])
        summed = own_part[at, :] + res[at, :].astype(f32)
        for i in range(n_col - 1):
            summed = summed + part_in[peer(i), at, :].astype(f32)
        total[at, :] = summed
        squares[at, :] = jnp.broadcast_to(jnp.sum(summed * summed, axis=1, keepdims=True), (rows, LANES))

    for i in range(chips):
        pos = (p + i) % chips
        done(row_slots(pos * 2 + 1 - core), hid_row.at[pos])

    tile = 16
    eight = 8 // hid_rows if hid_rows < 8 else 1
    per = tile // hid_rows

    def normalize(t, _):
        at = pl.ds(pl.multiple_of(t * tile, tile), tile)
        x = jnp.concatenate(
            [
                jnp.concatenate([hid[t * per + g + i].astype(f32) for i in range(eight)], axis=0)
                for g in range(0, per, eight)
            ],
            axis=0,
        )
        x = x * lax.rsqrt(jnp.mean(x * x, axis=1, keepdims=True) + norm_eps)
        normed[at, :] = x
        student[at, :] = (x * sgain[...]).astype(bf16)
        return 0

    lax.fori_loop(0, tokens // tile, normalize, 0)

    proj_copy.wait()
    predicted[...] = jnp.dot(student[...], proj[...], preferred_element_type=f32)
    gather_parts(0, main_at, main_rows)

    for b in range(tokens // LANES):
        lanes = slice(b * LANES, (b + 1) * LANES)
        row = jnp.transpose(squares[lanes, :])[0:1, :]
        sq_out[:, lanes] = row
        sq_in[me, :, lanes] = row

    def send_sq(i, _):
        d = (me + turn(devices) * (1 + i)) % devices
        remote(sq_out, sq_in.at[me], all_send.at[0], all_recv.at[0], (d // n_col, d % n_col)).start()
        return 0

    lax.fori_loop(0, devices - 1, send_sq, 0)

    both[0:tokens, :] = predicted[...].astype(bf16)
    both[tokens:, :] = (total[...] * tgain[...]).astype(bf16)
    step = 512

    def early(n, _):
        at = pl.ds(pl.multiple_of(n * step, step), step)
        back = lax.dot_general(
            both[...], proj[at, :], (((1,), (1,)), ((), ())), preferred_element_type=f32
        )
        x = normed[:, at]
        fixed[:, at] = jnp.sum(back[0:tokens, :] * x, axis=0, keepdims=True)
        normed[:, at] = back[tokens:, :] * x
        return 0

    lax.fori_loop(0, d_s // step, early, 0)

    others = sq_in.at[pl.ds(0, devices - 1)]
    done(others, all_recv.at[0])
    factor = lax.rsqrt(jnp.sum(sq_in[...], axis=0) / d_t + norm_eps)
    blocks = [slice(b * LANES, (b + 1) * LANES) for b in range(tokens // LANES)]
    scales = [jnp.transpose(jnp.broadcast_to(factor[:, lanes], (LANES, LANES))) for lanes in blocks]
    half = d_s // LANES // 2
    gp[:, half:half + 1, :] = jnp.zeros((2, 1, LANES), f32)
    give = remote(gp.at[1 - core], gp_in, pair_send.at[0], pair_recv.at[0], partner)
    for side in (1 - core, core):
        for q in range(half):
            lanes = pl.ds(pl.multiple_of((side * half + q) * LANES, LANES), LANES)
            moved = jnp.zeros((1, LANES), f32)
            for at, scale in zip(blocks, scales):
                moved = moved + jnp.sum(normed[at, lanes] * scale, axis=0, keepdims=True)
            gp[side, q:q + 1, :] = (fixed[:, lanes] - moved) * (1.0 / 64.0)
        if side is not core:
            give.start()
    loss_part = jnp.zeros((1, 1), f32)
    for at, scale in zip(blocks, scales):
        target = (total[at, :] * scale[:, 0:1] * tgain[...]).astype(bf16)
        difference = predicted[at, :] - target.astype(f32)
        loss_part = loss_part + jnp.sum(difference * difference, keepdims=True)
        error[at, :] = (difference * (1.0 / 64.0)).astype(bf16)

    give.wait_recv()
    place = p * n_col + c
    gs[...] = gp[core] + gp_in[...]
    gs[half:half + 1, :] = jnp.broadcast_to(loss_part, (1, LANES))
    gs_in[place] = gs[...]
    count = chips * n_col

    def send_gain(i, _):
        d = (place + turn(count) * (1 + i)) % count
        remote(
            gs, gs_in.at[place], all_send.at[1], all_recv.at[1], ((d // n_col) * 2 + core, d % n_col)
        ).start()
        return 0

    lax.fori_loop(0, count - 1, send_gain, 0)
    rest = gs_in.at[pl.ds(0, count - 1)]

    def project(i, _):
        at = pl.ds(pl.multiple_of(i * step, step), step)
        grad_out[at, :] = lax.dot_general(
            student[:, at], error[...], (((0,), (0,)), ((), ())), preferred_element_type=f32
        )
        return 0

    lax.fori_loop(0, d_s // step, project, 0)
    for k in range(CHUNKS):
        for way in range(2):
            sign = 1 - 2 * way
            for d in range(1, min(DIRECT, chips - 1) + 1):
                @pl.when(inside(p + sign * d))
                def _(way=way, d=d, k=k):
                    done(context.at[:, cols_of(k)], ctx_send.at[way, d - 1, k])
            for d in range(DIRECT, chips):
                pos = p - sign * d

                @pl.when(inside(pos) & inside(p + sign))
                def _(way=way, pos=pos, k=k):
                    done(block(pos, k), ctx_fwd.at[way, pos, k])
        for pos in range(chips):
            done(block(pos, k), ctx_side.at[pos, k])
    for i in range(chips - 1):
        done(hidden, hid_z.at[i])
    for i in range(n_col - 1):
        for pos in range(chips):
            done(slot(pos, c), hid_side.at[i, pos])
        done(res_part(peer(i)), col_send.at[0, i])
        done(part_out.at[i, main_at, :], col_send.at[1, i])
    for pos in range(chips):
        done(row_slots(pos * 2 + core), hid_pair.at[pos])
    done(others, all_send.at[0])
    give.wait_send()

    done(rest, all_recv.at[1])
    final[core] = jnp.sum(gs_in[...], axis=0)
    swap = remote(final.at[core], final.at[core], pair_send.at[1], pair_recv.at[1], partner)
    swap.start()
    done(rest, all_send.at[1])
    done(final.at[1 - core], pair_recv.at[1])
    loss_out[...] = (final[0, half:half + 1, :] + final[1, half:half + 1, :]) / (tokens * d_t)
    gain_out[0:half, :] = final[0, 0:half, :]
    gain_out[half:, :] = final[1, 0:half, :]
    swap.wait_send()


def store(grad, gain_in, loss_in, grad_out, gain_out, loss_out, sem):
    steps = sem.shape[0] - 2
    size = grad.shape[0] // steps
    copies = []
    for i in range(steps):
        rows = pl.ds(i * size, size)
        copies.append(pltpu.make_async_copy(grad.at[rows, :], grad_out.at[rows, :], sem.at[i]))
    copies.append(pltpu.make_async_copy(gain_in, gain_out, sem.at[steps]))
    copies.append(pltpu.make_async_copy(loss_in, loss_out, sem.at[steps + 1]))
    for copy in copies:
        copy.start()
    for copy in copies:
        copy.wait()


def store_call(grad, gain, loss, room):
    hbm = pl.BlockSpec(memory_space=pltpu.HBM)
    return pl.pallas_call(
        store,
        out_shape=tuple(jax.ShapeDtypeStruct(a.shape, a.dtype) for a in (grad, gain, loss)),
        in_specs=[pl.BlockSpec(memory_space=pltpu.VMEM), hbm, hbm],
        out_specs=(hbm,) * 3,
        scratch_shapes=[pltpu.SemaphoreType.DMA((STORES + 2,))],
        compiler_params=pltpu.CompilerParams(vmem_limit_bytes=room),
    )(pltpu.with_memory_space_constraint(grad, pltpu.VMEM), gain, loss)


def per_device(
    n_row, n_col,
    context, out_weight, residual, teacher_gain, student_hidden, student_gain, projector,
):
    devices = n_row * n_col
    chips = n_row // 2
    tokens = context.shape[0] * n_row
    d_s, width = projector.shape
    half = d_s // LANES // 2
    f32, bf16 = jnp.float32, jnp.bfloat16
    anywhere = pl.BlockSpec(memory_space=pl.ANY)
    vmem = pl.BlockSpec(memory_space=pltpu.VMEM)
    dma = pltpu.SemaphoreType.DMA
    room = 67_000_000 - d_s * width * 4
    grad_proj, grad_gain, loss = pl.pallas_call(
        functools.partial(body, n_row, n_col),
        out_shape=(
            pltpu.VMEM((d_s, width), f32),
            jax.ShapeDtypeStruct((2 * half, LANES), f32),
            jax.ShapeDtypeStruct((1, LANES), f32),
        ),
        in_specs=[anywhere, anywhere, anywhere, vmem, anywhere, vmem, anywhere],
        out_specs=(vmem, vmem, vmem),
        scratch_shapes=[
            pltpu.VMEM((tokens, d_s), bf16),
            pltpu.VMEM((tokens, width), bf16),
            pltpu.VMEM((tokens, context.shape[1]), bf16),
            pltpu.VMEM(out_weight.shape, bf16),
            pltpu.VMEM((d_s, width), bf16),
            pltpu.VMEM((tokens, width), f32),
            pltpu.VMEM((n_col - 1, tokens, width), bf16),
            pltpu.VMEM((n_col, tokens, width), bf16),
            pltpu.VMEM((tokens, width), bf16),
            pltpu.VMEM((devices,) + student_hidden.shape, bf16),
            pltpu.VMEM((tokens, d_s), f32),
            pltpu.VMEM((1, d_s), f32),
            pltpu.VMEM((1, width), f32),
            pltpu.VMEM((tokens, width), f32),
            pltpu.VMEM((tokens, width), f32),
            pltpu.VMEM((2 * tokens, width), bf16),
            pltpu.VMEM((tokens, LANES), f32),
            pltpu.VMEM((1, tokens), f32),
            pltpu.VMEM((devices, 1, tokens), f32),
            pltpu.VMEM((1, d_s), f32),
            pltpu.VMEM((2, half + 1, LANES), f32),
            pltpu.VMEM((half + 1, LANES), f32),
            pltpu.VMEM((half + 1, LANES), f32),
            pltpu.VMEM((chips * n_col, half + 1, LANES), f32),
            pltpu.VMEM((2, half + 1, LANES), f32),
            dma((6,)),
            dma((CHUNKS,)),
            dma((2, DIRECT, CHUNKS)),
            dma((2, chips, CHUNKS)),
            dma((chips, CHUNKS)),
            dma((n_row, CHUNKS)),
            dma((chips,)),
            dma((n_col, chips)),
            dma((chips,)),
            dma((chips, n_col)),
            dma((chips,)),
            dma((3, n_col)),
            dma((3, n_col)),
            dma((2,)),
            dma((2,)),
            dma((2,)),
            dma((2,)),
        ],
        compiler_params=pltpu.CompilerParams(
            collective_id=0, has_side_effects=True, vmem_limit_bytes=room
        ),
    )(
        context, out_weight, residual, teacher_gain.reshape(-1, LANES), student_hidden,
        student_gain.reshape(-1, LANES), projector,
    )
    grad_proj, grad_gain, loss = store_call(grad_proj, grad_gain, loss, room)
    return (grad_proj, grad_gain.reshape(-1), loss[0, 0])


def solution(mesh):
    placed = (
        P("row", "col"),
        P("col", "row"),
        P("col", "row"),
        P(),
        P(("row", "col"), None),
        P(),
        P(None, ("row", "col")),
    )
    return jax.shard_map(
        functools.partial(per_device, mesh.shape["row"], mesh.shape["col"]),
        mesh=mesh,
        in_specs=placed,
        out_specs=(P(None, ("row", "col")), P(), P()),
        check_vma=False,
    )
```
